256 devices in a mesh: gx: 16 (over x, y_lo, core), gy: 16 (over y_hi, z).
Axes of the slice: x: 4, y: 4 (y_hi: 2, y_lo: 2; y = y_hi * 2 + y_lo), z: 8, core: 2. Of those that a mesh axis runs over, the one named last changes fastest.
Arguments:
- wave_fields: float32 [9, 32, 128, 2048], P(None, None, 'gy', 'gx'), may hold values from -6 to 6
- lame_lambda: float32 [32, 128, 2048], P(None, 'gy', 'gx'), may hold values from 0.5 to 1
- shear_modulus: float32 [32, 128, 2048], P(None, 'gy', 'gx'), may hold values from 0.3 to 0.7
- buoyancy: float32 [32, 128, 2048], P(None, 'gy', 'gx'), may hold values from 0.5 to 1
- ocean_state: float32 [3, 128, 2048], P(None, 'gy', 'gx'), may hold values from -6 to 6
- water_depth: float32 [128, 2048], P('gy', 'gx'), may hold values from 0.5 to 2
- seafloor_index: int32 [128, 2048], P('gy', 'gx'), may hold values from 0 to 15
- wet_mask: int32 [128, 2048], P('gy', 'gx'), may hold values 0 or 1
Outputs:
- wave_out: float32 [9, 32, 128, 2048], P(None, None, 'gy', 'gx')
- ocean_out: float32 [3, 128, 2048], P(None, 'gy', 'gx')
The draws below stay inside these ranges and needn't reach their ends.
All inputs are finite; a program needn't handle non-finite values. No bound on the sum of `wet_mask` on one device may be relied on, other than what follows from the above.
Results may differ from the reference program's by a relative error of at most 0.0001.
Values sent between devices are 32-bit elements; how exact they have to be, the bound alone decides.
A program may use at most 64 MiB of HBM per device.

```python
import math
import jax
import jax.numpy as jnp

CZ = 32
STEPS = 2
NX = 2048
NY = 128


def with_ends(array, own_key, least, top_value):
    dims = array.shape
    place = [jax.random.randint(jax.random.fold_in(own_key, axis), (), 0, dims[axis]) for axis in range(len(dims))]
    array = array.at[tuple(place)].set(least)
    longest = dims.index(max(dims))
    place[longest] = (place[longest] + 1) % dims[longest]
    return array.at[tuple(place)].set(top_value)


def block_scale(stream_key, dims, shards, smallest, top_value):
    gain, own = 1.0, jax.random.fold_in(stream_key, 6)
    for axis_at, shards_of in shards:
        draws = jnp.exp(jax.random.uniform(jax.random.fold_in(own, axis_at), (shards_of,), jnp.float32, smallest / len(shards), top_value / len(shards)))
        gain = gain * jnp.repeat(draws, dims[axis_at] // shards_of).reshape([-1 if axis == axis_at else 1 for axis in range(len(dims))])
    return gain


def scatter_about(own_key, shape, scale, most, shards=(), kind=jnp.bfloat16):
    array = scale * jax.random.normal(own_key, shape, jnp.float32)
    if shards:
        array = array * block_scale(own_key, shape, shards, -0.22, 0.18)
    return jnp.clip(array, -most, most).astype(kind)


def setup_inputs(seed: int = 0) -> dict:
    streams_of = jax.random.split(jax.random.key(seed), 9)
    wave_fields = scatter_about(streams_of[0], (9, CZ, NY, NX), 1.0, 6.0, ((2, 16), (3, 16)), jnp.float32)
    lame_lambda = jnp.clip(0.5 + 0.5 * jax.random.uniform(streams_of[1], (CZ, NY, NX), jnp.float32) ** block_scale(streams_of[1], (CZ, NY, NX), ((1, 16), (2, 16)), -0.2, 0.2), 0.5, 1.0)
    shear_modulus = jnp.clip(0.3 + 0.39999998 * jax.random.uniform(streams_of[2], (CZ, NY, NX), jnp.float32) ** block_scale(streams_of[2], (CZ, NY, NX), ((1, 16), (2, 16)), -0.2, 0.2), 0.3, 0.7)
    buoyancy = jnp.clip(0.5 + 0.5 * jax.random.uniform(streams_of[3], (CZ, NY, NX), jnp.float32) ** block_scale(streams_of[3], (CZ, NY, NX), ((1, 16), (2, 16)), -0.2, 0.2), 0.5, 1.0)
    ocean_state = scatter_about(streams_of[4], (3, NY, NX), 1.0, 6.0, ((1, 16), (2, 16)), jnp.float32)
    water_depth = jnp.clip(jnp.exp(math.log(2.0) - 1.3862944 * jax.random.uniform(streams_of[5], (NY, NX), jnp.float32) ** block_scale(streams_of[5], (NY, NX), ((0, 16), (1, 16)), -0.2, 0.2)), 0.5, 2.0)
    seafloor_index = with_ends(jax.random.randint(streams_of[6], (NY, NX), 0, CZ // 2), jax.random.fold_in(streams_of[6], 1), 0, (CZ // 2) - 1).astype(jnp.int32)
    wet_mask = with_ends((jax.random.randint(streams_of[7], (NY, NX), 0, 4) < 3).astype(jnp.int32), jax.random.fold_in(streams_of[7], 1), 0, 1)
    return dict(wave_fields=wave_fields, lame_lambda=lame_lambda, shear_modulus=shear_modulus, buoyancy=buoyancy, ocean_state=ocean_state, water_depth=water_depth, seafloor_index=seafloor_index, wet_mask=wet_mask)


coef_near = 9.0 / 8.0
coef_far = -1.0 / 24.0
courant = 0.3
ocean_rate = 0.3
uplift = 0.5
loading = 0.5
viscous = 0.1


def differ(padded, direction, margins, forward):
    extent = padded.shape

    def sample(offset):
        selector = []
        for dimension in range(3):
            margin = margins[dimension]
            if dimension == direction:
                selector.append(slice(margin + offset, extent[dimension] - margin + offset))
            else:
                selector.append(slice(margin, extent[dimension] - margin))
        return padded[tuple(selector)]

    if forward:
        return coef_near * (sample(1) - sample(0)) + coef_far * (sample(2) - sample(-1))
    return coef_near * (sample(0) - sample(-1)) + coef_far * (sample(1) - sample(-2))


def advance_velocity(velocity, stress_pad, buoyancy, margins):
    stress_xx, stress_yy, stress_zz = stress_pad[0], stress_pad[1], stress_pad[2]
    stress_xy, stress_xz, stress_yz = stress_pad[3], stress_pad[4], stress_pad[5]
    accel_x = differ(stress_xx, 2, margins, True) + differ(stress_xy, 1, margins, False) + differ(stress_xz, 0, margins, False)
    accel_y = differ(stress_xy, 2, margins, False) + differ(stress_yy, 1, margins, True) + differ(stress_yz, 0, margins, False)
    accel_z = differ(stress_xz, 2, margins, False) + differ(stress_yz, 1, margins, False) + differ(stress_zz, 0, margins, True)
    return jnp.stack([velocity[0] + courant * buoyancy * accel_x,
                      velocity[1] + courant * buoyancy * accel_y,
                      velocity[2] + courant * buoyancy * accel_z])


def advance_stress(stress, velocity_pad, lame, shear, margins):
    speed_x, speed_y, speed_z = velocity_pad[0], velocity_pad[1], velocity_pad[2]
    strain_x = differ(speed_x, 2, margins, False)
    strain_y = differ(speed_y, 1, margins, False)
    strain_z = differ(speed_z, 0, margins, False)
    trace = strain_x + strain_y + strain_z
    shear_xy = differ(speed_x, 1, margins, True) + differ(speed_y, 2, margins, True)
    shear_xz = differ(speed_x, 0, margins, True) + differ(speed_z, 2, margins, True)
    shear_yz = differ(speed_y, 0, margins, True) + differ(speed_z, 1, margins, True)
    return jnp.stack([stress[0] + courant * (lame * trace + 2.0 * shear * strain_x),
                      stress[1] + courant * (lame * trace + 2.0 * shear * strain_y),
                      stress[2] + courant * (lame * trace + 2.0 * shear * strain_z),
                      stress[3] + courant * shear * shear_xy,
                      stress[4] + courant * shear * shear_xz,
                      stress[5] + courant * shear * shear_yz])


def ocean_level(level, flux_pad, vertical, onehot, wet):
    seafloor = jnp.sum(vertical * onehot, axis=0)
    east = flux_pad[0]
    north = flux_pad[1]
    spread = 0.5 * (east[1:-1, 2:] - east[1:-1, :-2]) + 0.5 * (north[2:, 1:-1] - north[:-2, 1:-1])
    return level + wet * (uplift * seafloor - ocean_rate * spread)


def ocean_flux(fluxes, flux_pad, level_pad, depth, wet):
    slope_x = 0.5 * (level_pad[1:-1, 2:] - level_pad[1:-1, :-2])
    slope_y = 0.5 * (level_pad[2:, 1:-1] - level_pad[:-2, 1:-1])
    laplace = flux_pad[:, 1:-1, 2:] + flux_pad[:, 1:-1, :-2] + flux_pad[:, 2:, 1:-1] + flux_pad[:, :-2, 1:-1] - 4.0 * fluxes
    east = wet * (fluxes[0] - ocean_rate * depth * slope_x + viscous * laplace[0])
    north = wet * (fluxes[1] - ocean_rate * depth * slope_y + viscous * laplace[1])
    return jnp.stack([east, north])


def reference(wave_fields, lame_lambda, shear_modulus, buoyancy, ocean_state, water_depth, seafloor_index, wet_mask):
    wet = wet_mask.astype(jnp.float32)
    layers = jnp.arange(wave_fields.shape[1], dtype=jnp.int32)
    onehot = (layers[:, None, None] == seafloor_index[None, :, :]).astype(jnp.float32)
    fields = wave_fields
    ocean = ocean_state
    for number in range(STEPS):
        velocity = fields[0:3]
        stress = fields[3:9]
        stress_pad = jnp.pad(stress, ((0, 0), (2, 2), (2, 2), (2, 2)))
        velocity = advance_velocity(velocity, stress_pad, buoyancy, (2, 2, 2))
        velocity_pad = jnp.pad(velocity, ((0, 0), (2, 2), (2, 2), (2, 2)))
        stress = advance_stress(stress, velocity_pad, lame_lambda, shear_modulus, (2, 2, 2))
        flux_pad = jnp.pad(ocean[1:3], ((0, 0), (1, 1), (1, 1)))
        level = ocean_level(ocean[0], flux_pad, velocity[2], onehot, wet)
        level_pad = jnp.pad(level, ((1, 1), (1, 1)))
        fluxes = ocean_flux(ocean[1:3], flux_pad, level_pad, water_depth, wet)
        pressed = stress[2] - loading * onehot * (wet * level)[None, :, :]
        stress = jnp.concatenate([stress[0:2], pressed[None], stress[3:6]], axis=0)
        fields = jnp.concatenate([velocity, stress], axis=0)
        ocean = jnp.concatenate([level[None], fluxes], axis=0)
    return fields, ocean
```

```python
import functools

import jax
import jax.numpy as jnp
from jax import lax
from jax.experimental import pallas as pl
from jax.experimental.pallas import tpu as pltpu
from jax.sharding import PartitionSpec as P

STEPS = 2
CHUNK = 8

near = 9.0 / 8.0
far = -1.0 / 24.0
courant = 0.3
ocean_rate = 0.3
uplift = 0.5
loading = 0.5
viscous = 0.1

YY, XY, YZ, XX, XZ, ZZ = range(6)
STRESS_SOURCE = (4, 6, 8, 3, 7, 5)


def turned(tile, shift, axis):
    return pltpu.roll(tile, shift % tile.shape[axis], axis)


def kernel(
    counts,
    fields_ref,
    lame_ref,
    shear_ref,
    buoy_ref,
    ocean_ref,
    depth_ref,
    index_ref,
    wet_ref,
    wave_out,
    ocean_out,
    stress_a,
    speed_a,
    lame,
    shear,
    buoy,
    ocean,
    depth,
    index,
    wet_i,
    stress_b,
    stress_c,
    speed_b,
    speed_c,
    halo_y,
    halo_o,
    pack,
    halo_x,
    edges,
    result_o,
    load_sem,
    out_sem,
    send_y,
    recv_y,
    send_o,
    recv_o,
    send_x,
    recv_x,
):
    count_x, count_y = counts
    at_x, at_y = lax.axis_index("gx"), lax.axis_index("gy")
    layers = fields_ref.shape[1]
    chunks = layers // CHUNK
    tile = (8, 128)

    has_y = (at_y < count_y - 1, at_y > 0)
    has_x = (at_x < count_x - 1, at_x > 0)
    to_y = ({"gy": jnp.minimum(at_y + 1, count_y - 1)}, {"gy": jnp.maximum(at_y - 1, 0)})
    to_x = ({"gx": jnp.minimum(at_x + 1, count_x - 1)}, {"gx": jnp.maximum(at_x - 1, 0)})

    loads = []

    def load(source, target):
        copy = pltpu.make_async_copy(source, target, load_sem.at[len(loads)])
        copy.start()
        loads.append(copy)

    for place, source in enumerate(STRESS_SOURCE):
        load(fields_ref.at[source], stress_a.at[place, pl.ds(2, layers)])
    load(ocean_ref, ocean)
    load(fields_ref.at[pl.ds(0, 3)], speed_a)
    load(buoy_ref, buoy)
    load(lame_ref, lame)
    load(shear_ref, shear)
    load(depth_ref, depth)
    load(index_ref, index)
    load(wet_ref, wet_i)

    none = jnp.zeros(tile, jnp.float32)
    for direction in range(2):
        @pl.when(jnp.logical_not(has_y[1 - direction]))
        def _():
            rows = slice(6, 8) if direction == 0 else slice(0, 2)

            def clear(z, carry):
                for number in range(2 * STEPS):
                    for field in range(3):
                        halo_y[number, field, z, rows, :] = jnp.zeros((2, 128), jnp.float32)
                return carry

            lax.fori_loop(0, layers, clear, 0)
            for number in range(2 * STEPS):
                for field in range(2):
                    row = slice(7, 8) if direction == 0 else slice(0, 1)
                    halo_o[number, field, row, :] = jnp.zeros((1, 128), jnp.float32)

        @pl.when(jnp.logical_not(has_x[1 - direction]))
        def _():
            for number in range(2 * STEPS):
                for place in range(4):
                    halo_x[number, direction, place] = none

    barrier = pltpu.get_barrier_semaphore()
    for has, to in ((has_y, to_y), (has_x, to_x)):
        for direction in range(2):

            @pl.when(has[direction])
            def _():
                pl.semaphore_signal(barrier, inc=1, device_id=to[direction])

    for stress in (stress_a, stress_b):
        for field in (YZ, XZ, ZZ):
            for z in (0, 1, layers + 2, layers + 3):
                stress[field, z] = none
    for speed in (speed_b, speed_c):
        for field in range(3):
            for z in (0, 1, layers + 2, layers + 3):
                speed[field, z] = none

    row_at = lax.broadcasted_iota(jnp.int32, tile, 0)
    lane_at = lax.broadcasted_iota(jnp.int32, tile, 1)
    group_at = lane_at // 4

    def rows_copy(number, source, direction, chunk):
        rows = pl.ds(6, 2) if direction == 0 else pl.ds(0, 2)
        return pltpu.make_async_remote_copy(
            source.at[pl.ds(0, 3), pl.ds(2 + chunk * CHUNK, CHUNK), rows, :],
            halo_y.at[number, :, pl.ds(chunk * CHUNK, CHUNK), rows, :],
            send_y.at[number, direction, chunk],
            recv_y.at[number, direction, chunk],
            device_id=to_y[direction],
        )

    def ocean_copy(number, direction):
        count = 2 if number % 2 == 0 else 1
        row = pl.ds(7, 1) if direction == 0 else pl.ds(0, 1)
        return pltpu.make_async_remote_copy(
            edges.at[number, pl.ds(0, count), row, :],
            halo_o.at[number, pl.ds(0, count), row, :],
            send_o.at[number, direction],
            recv_o.at[number, direction],
            device_id=to_y[direction],
        )

    def columns_copy(number, direction):
        return pltpu.make_async_remote_copy(
            pack.at[number],
            halo_x.at[number, direction],
            send_x.at[number, direction],
            recv_x.at[number, direction],
            device_id=to_x[direction],
        )

    def begin(make, has):
        for direction in range(2):

            @pl.when(has[direction])
            def _():
                make(direction).start()

    def arrive(make, has):
        for direction in range(2):

            @pl.when(has[1 - direction])
            def _():
                make(direction).wait_recv()

    def leave(make, has):
        for direction in range(2):

            @pl.when(has[direction])
            def _():
                make(direction).wait_send()

    def packed(held, tile_z, inner):
        return jnp.where(group_at == inner, turned(tile_z, 2 + 4 * inner, 1), held)

    def settle(held, part, chunk):
        moved = pltpu.roll(part, chunk * (4 * CHUNK), 1)
        return jnp.where(lane_at // (4 * CHUNK) == chunk, moved, held)

    def columns(number, place):
        low, high = halo_x[number, 0, place], halo_x[number, 1, place]
        return jnp.where(lane_at % 4 < 2, low, high)

    def chunk_columns(number, place, chunk):
        return pltpu.roll(columns(number, place), (128 - chunk * (4 * CHUNK)) % 128, 1)

    def unpacked(part, inner):
        return turned(part, -(2 + 4 * inner), 1)

    def shifted(tile_z, halo, axis, by):
        at, size = (row_at, 8) if axis == 0 else (lane_at, 128)
        from_halo = at >= size - by if by > 0 else at < -by
        return turned(jnp.where(from_halo, halo, tile_z), by, axis)

    def differ(tile_z, halo, axis, forward):
        before = shifted(tile_z, halo, axis, 1)
        after = shifted(tile_z, halo, axis, -1)
        if forward:
            after_two = shifted(tile_z, halo, axis, -2)
            return near * (after - tile_z) + far * (after_two - before)
        before_two = shifted(tile_z, halo, axis, 2)
        return near * (tile_z - before) + far * (after - before_two)

    def differ_z(ref, field, z, forward):
        at = [ref[field, z + 2 + k] for k in ((-1, 0, 1, 2) if forward else (-2, -1, 0, 1))]
        return near * (at[2] - at[1]) + far * (at[3] - at[0])

    def zero_pack():
        return (none, none, none)

    def pack_stress(stress, chunk, held):
        parts = [none, none, none]
        for inner in range(CHUNK):
            for place, field in enumerate((XX, XY, XZ)):
                parts[place] = packed(parts[place], stress[field, chunk * CHUNK + inner + 2], inner)
        return tuple(settle(h, p, chunk) for h, p in zip(held, parts))

    def finish_pack(number, held, extra):
        for place in range(3):
            pack[number, place] = held[place]
        last = none
        for place, item in enumerate(extra):
            last = packed(last, item, place)
        pack[number, 3] = last

    def velocity_stage(number, stress, speed_old, speed_new):
        arrive(functools.partial(columns_copy, number), has_x)

        def body(chunk, held):
            arrive(lambda d: rows_copy(number, stress, d, chunk), has_y)
            side = [chunk_columns(number, place, chunk) for place in range(3)]
            parts = [none, none, none]
            for inner in range(CHUNK):
                z = chunk * CHUNK + inner
                sxx, sxy, sxz = stress[XX, z + 2], stress[XY, z + 2], stress[XZ, z + 2]
                syy, syz = stress[YY, z + 2], stress[YZ, z + 2]
                hx = [unpacked(s, inner) for s in side]
                ax = (
                    differ(sxx, hx[0], 1, True)
                    + differ(sxy, halo_y[number, XY, z], 0, False)
                    + differ_z(stress, XZ, z, False)
                )
                ay = (
                    differ(sxy, hx[1], 1, False)
                    + differ(syy, halo_y[number, YY, z], 0, True)
                    + differ_z(stress, YZ, z, False)
                )
                az = (
                    differ(sxz, hx[2], 1, False)
                    + differ(syz, halo_y[number, YZ, z], 0, False)
                    + differ_z(stress, ZZ, z, True)
                )
                rate = courant * buoy[z]
                for field, push in enumerate((ax, ay, az)):
                    old = speed_old[field, z] if speed_old is speed_a else speed_old[field, z + 2]
                    new = old + rate * push
                    speed_new[field, z + 2] = new
                    parts[field] = packed(parts[field], new, inner)
            begin(lambda d: rows_copy(number + 1, speed_new, d, chunk), has_y)
            return tuple(settle(h, p, chunk) for h, p in zip(held, parts))

        return lax.fori_loop(0, chunks, body, zero_pack())

    def stress_stage(number, speed, stress_old, write, send):
        arrive(functools.partial(columns_copy, number), has_x)

        def body(chunk, held):
            arrive(lambda d: rows_copy(number, speed, d, chunk), has_y)
            side = [chunk_columns(number, place, chunk) for place in range(3)]
            parts = [none, none, none]
            for inner in range(CHUNK):
                z = chunk * CHUNK + inner
                vx, vy, vz = speed[0, z + 2], speed[1, z + 2], speed[2, z + 2]
                hx = [unpacked(s, inner) for s in side]
                hy = [halo_y[number, field, z] for field in range(3)]
                strain_x = differ(vx, hx[0], 1, False)
                strain_y = differ(vy, hy[1], 0, False)
                strain_z = differ_z(speed, 2, z, False)
                shear_xy = differ(vx, hy[0], 0, True) + differ(vy, hx[1], 1, True)
                shear_xz = differ_z(speed, 0, z, True) + differ(vz, hx[2], 1, True)
                shear_yz = differ_z(speed, 1, z, True) + differ(vz, hy[2], 0, True)
                rate = courant * shear[z]
                bulk = (courant * lame[z]) * (strain_x + strain_y + strain_z)
                twice = 2.0 * rate
                press = jnp.where(index[...] == z, edges[number, 2], 0.0)
                new = {
                    XX: stress_old[XX, z + 2] + (bulk + twice * strain_x),
                    YY: stress_old[YY, z + 2] + (bulk + twice * strain_y),
                    ZZ: stress_old[ZZ, z + 2] + (bulk + twice * strain_z) - press,
                    XY: stress_old[XY, z + 2] + rate * shear_xy,
                    XZ: stress_old[XZ, z + 2] + rate * shear_xz,
                    YZ: stress_old[YZ, z + 2] + rate * shear_yz,
                }
                write(new, z)
                if send:
                    for place, field in enumerate((XX, XY, XZ)):
                        parts[place] = packed(parts[place], new[field], inner)
            if send:
                begin(lambda d: rows_copy(number + 1, stress_b, d, chunk), has_y)
                return tuple(settle(h, p, chunk) for h, p in zip(held, parts))
            out_copy(chunk).start()
            return held

        return lax.fori_loop(0, chunks, body, zero_pack())

    def out_copy(chunk):
        layer = pl.ds(chunk * CHUNK, CHUNK)
        return pltpu.make_async_copy(
            stress_c.at[:, layer], wave_out.at[pl.ds(3, 6), layer], out_sem.at[chunk]
        )

    def centred(tile_o, halo, axis):
        return 0.5 * (shifted(tile_o, halo, axis, -1) - shifted(tile_o, halo, axis, 1))

    def around(tile_o, rows, cols):
        return (
            shifted(tile_o, cols, 1, -1)
            + shifted(tile_o, cols, 1, 1)
            + shifted(tile_o, rows, 0, -1)
            + shifted(tile_o, rows, 0, 1)
            - 4.0 * tile_o
        )

    def level_stage(number, speed, level, flux_x, flux_y):
        arrive(functools.partial(ocean_copy, number), has_y)
        side = columns(number, 3)
        rows_y = halo_o[number, 1]
        seafloor = none
        for z in range(layers // 2):
            seafloor = seafloor + jnp.where(index[...] == z, speed[2, z + 2], 0.0)
        spread = centred(flux_x, unpacked(side, 0), 1) + centred(flux_y, rows_y, 0)
        wet = wet_i[...].astype(jnp.float32)
        level = level + wet * (uplift * seafloor - ocean_rate * spread)
        edges[number + 1, 0] = level
        edges[number + 1, 2] = loading * (wet * level)
        begin(functools.partial(ocean_copy, number + 1), has_y)
        return level

    def flux_stage(number, level, flux_x, flux_y):
        arrive(functools.partial(ocean_copy, number + 1), has_y)
        side = columns(number, 3)
        level_side = unpacked(columns(number + 1, 3), 0)
        slope_x = centred(level, level_side, 1)
        slope_y = centred(level, halo_o[number + 1, 0], 0)
        wet = wet_i[...].astype(jnp.float32)
        around_x = around(flux_x, halo_o[number, 0], unpacked(side, 0))
        around_y = around(flux_y, halo_o[number, 1], unpacked(side, 1))
        pull = ocean_rate * depth[...]
        return (
            wet * (flux_x - pull * slope_x + viscous * around_x),
            wet * (flux_y - pull * slope_y + viscous * around_y),
        )

    def write_middle(new, z):
        for field, value in new.items():
            stress_b[field, z + 2] = value

    def write_last(new, z):
        for field, value in new.items():
            stress_c[STRESS_SOURCE[field] - 3, z] = value

    for copy in loads[:7]:
        copy.wait()
    level, flux_x, flux_y = ocean[0], ocean[1], ocean[2]
    held = lax.fori_loop(
        0, chunks, lambda chunk, held: pack_stress(stress_a, chunk, held), zero_pack()
    )
    finish_pack(0, held, (flux_x, flux_y))
    edges[0, 0] = flux_x
    edges[0, 1] = flux_y
    peers = sum(has.astype(jnp.int32) for has in (*has_y, *has_x))
    pl.semaphore_wait(barrier, peers)

    for chunk in range(chunks):
        begin(lambda d: rows_copy(0, stress_a, d, chunk), has_y)
    begin(functools.partial(columns_copy, 0), has_x)
    begin(functools.partial(ocean_copy, 0), has_y)
    for copy in loads[7:]:
        copy.wait()

    speeds = (speed_a, speed_b, speed_c)
    stresses = (stress_a, stress_b)
    for step in range(STEPS):
        number = 2 * step
        last = step == STEPS - 1
        held = velocity_stage(number, stresses[step], speeds[step], speeds[step + 1])
        new_level = level_stage(number, speeds[step + 1], level, flux_x, flux_y)
        finish_pack(number + 1, held, (new_level,))
        begin(functools.partial(columns_copy, number + 1), has_x)
        if last:
            speed_out = pltpu.make_async_copy(
                speed_c.at[:, pl.ds(2, layers)], wave_out.at[pl.ds(0, 3)], out_sem.at[chunks]
            )
            speed_out.start()
        held = stress_stage(
            number + 1,
            speeds[step + 1],
            stresses[step],
            write_last if last else write_middle,
            not last,
        )
        flux_x, flux_y = flux_stage(number, new_level, flux_x, flux_y)
        level = new_level
        if not last:
            edges[number + 2, 0] = flux_x
            edges[number + 2, 1] = flux_y
            finish_pack(number + 2, held, (flux_x, flux_y))
            begin(functools.partial(columns_copy, number + 2), has_x)
            begin(functools.partial(ocean_copy, number + 2), has_y)

    result_o[0] = level
    result_o[1] = flux_x
    result_o[2] = flux_y
    level_out = pltpu.make_async_copy(result_o, ocean_out, out_sem.at[chunks + 1])
    level_out.start()

    sources = (stress_a, speed_b, stress_b, speed_c)
    for number in range(2 * STEPS):

        def drain(chunk, carry):
            leave(lambda d: rows_copy(number, sources[number], d, chunk), has_y)
            return carry

        lax.fori_loop(0, chunks, drain, 0)
        leave(functools.partial(ocean_copy, number), has_y)
        leave(functools.partial(columns_copy, number), has_x)
    for chunk in range(chunks):
        out_copy(chunk).wait()
    speed_out.wait()
    level_out.wait()


def solution(mesh):
    counts = (mesh.shape["gx"], mesh.shape["gy"])

    def local(*arrays):
        fields, ocean = arrays[0], arrays[4]
        layers = fields.shape[1]
        chunks = layers // CHUNK
        f32, dma = jnp.float32, pltpu.SemaphoreType.DMA
        rounds = 2 * STEPS
        cube = (layers, 8, 128)
        padded = (layers + 4, 8, 128)
        return pl.pallas_call(
            functools.partial(kernel, counts),
            out_shape=(
                jax.ShapeDtypeStruct(fields.shape, f32),
                jax.ShapeDtypeStruct(ocean.shape, f32),
            ),
            in_specs=[pl.BlockSpec(memory_space=pl.ANY)] * 8,
            out_specs=(pl.BlockSpec(memory_space=pl.ANY), pl.BlockSpec(memory_space=pl.ANY)),
            scratch_shapes=[
                pltpu.VMEM((6, *padded), f32),
                pltpu.VMEM((3, *cube), f32),
                pltpu.VMEM(cube, f32),
                pltpu.VMEM(cube, f32),
                pltpu.VMEM(cube, f32),
                pltpu.VMEM((3, 8, 128), f32),
                pltpu.VMEM((8, 128), f32),
                pltpu.VMEM((8, 128), jnp.int32),
                pltpu.VMEM((8, 128), jnp.int32),
                pltpu.VMEM((6, *padded), f32),
                pltpu.VMEM((6, *cube), f32),
                pltpu.VMEM((3, *padded), f32),
                pltpu.VMEM((3, *padded), f32),
                pltpu.VMEM((rounds, 3, *cube), f32),
                pltpu.VMEM((rounds, 2, 8, 128), f32),
                pltpu.VMEM((rounds, 4, 8, 128), f32),
                pltpu.VMEM((rounds, 2, 4, 8, 128), f32),
                pltpu.VMEM((rounds, 3, 8, 128), f32),
                pltpu.VMEM((3, 8, 128), f32),
                dma((14,)),
                dma((chunks + 2,)),
                dma((rounds, 2, chunks)),
                dma((rounds, 2, chunks)),
                dma((rounds, 2)),
                dma((rounds, 2)),
                dma((rounds, 2)),
                dma((rounds, 2)),
            ],
            compiler_params=pltpu.CompilerParams(collective_id=0, has_side_effects=True),
            name="waves",
        )(*arrays)

    flat = P("gy", "gx")
    deep = P(None, "gy", "gx")
    in_specs = (P(None, None, "gy", "gx"), deep, deep, deep, deep, flat, flat, flat)
    out_specs = (P(None, None, "gy", "gx"), deep)
    return jax.shard_map(local, mesh=mesh, in_specs=in_specs, out_specs=out_specs, check_vma=False)
```

```python
import functools

import jax
import jax.numpy as jnp
from jax import lax
from jax.experimental import pallas as pl
from jax.experimental.pallas import tpu as pltpu
from jax.sharding import PartitionSpec as P

STEPS = 2
CHUNK = 8

near = 9.0 / 8.0
far = -1.0 / 24.0
courant = 0.3
ocean_rate = 0.3
uplift = 0.5
loading = 0.5
viscous = 0.1

YY, XY, YZ, XX, XZ, ZZ = range(6)
STRESS_SOURCE = (4, 6, 8, 3, 7, 5)


def turned(tile, shift, axis):
    return pltpu.roll(tile, shift % tile.shape[axis], axis)


def kernel(
    counts,
    fields_ref,
    lame_ref,
    shear_ref,
    buoy_ref,
    ocean_ref,
    depth_ref,
    index_ref,
    wet_ref,
    wave_out,
    ocean_out,
    stress_a,
    speed_a,
    lame,
    shear,
    buoy,
    ocean,
    depth,
    index,
    wet_i,
    stress_b,
    speed_b,
    speed_c,
    halo_y,
    halo_o,
    pack,
    halo_x,
    edges,
    load_sem,
    send_y,
    recv_y,
    send_o,
    recv_o,
    send_x,
    recv_x,
):
    count_x, count_y = counts
    at_x, at_y = lax.axis_index("gx"), lax.axis_index("gy")
    layers = fields_ref.shape[1]
    chunks = layers // CHUNK
    tile = (8, 128)

    has_y = (at_y < count_y - 1, at_y > 0)
    has_x = (at_x < count_x - 1, at_x > 0)
    to_y = ({"gy": jnp.minimum(at_y + 1, count_y - 1)}, {"gy": jnp.maximum(at_y - 1, 0)})
    to_x = ({"gx": jnp.minimum(at_x + 1, count_x - 1)}, {"gx": jnp.maximum(at_x - 1, 0)})

    barrier = pltpu.get_barrier_semaphore()
    for has, to in ((has_y, to_y), (has_x, to_x)):
        for direction in range(2):

            @pl.when(has[direction])
            def _():
                pl.semaphore_signal(barrier, inc=1, device_id=to[direction])

    loads = []

    def load(source, target):
        copy = pltpu.make_async_copy(source, target, load_sem.at[len(loads)])
        copy.start()
        loads.append(copy)

    for place, source in enumerate(STRESS_SOURCE):
        load(fields_ref.at[source], stress_a.at[place, pl.ds(2, layers)])
    load(ocean_ref, ocean)
    load(fields_ref.at[pl.ds(0, 3)], speed_a)
    load(buoy_ref, buoy)
    load(lame_ref, lame)
    load(shear_ref, shear)
    load(depth_ref, depth)
    load(index_ref, index)
    load(wet_ref, wet_i)

    none = jnp.zeros(tile, jnp.float32)
    for direction in range(2):
        @pl.when(jnp.logical_not(has_y[1 - direction]))
        def _():
            rows = slice(6, 8) if direction == 0 else slice(0, 2)

            def clear(z, carry):
                for number in range(2 * STEPS):
                    for field in range(3):
                        halo_y[number, field, z, rows, :] = jnp.zeros((2, 128), jnp.float32)
                return carry

            lax.fori_loop(0, layers, clear, 0)
            for number in range(2 * STEPS):
                for field in range(2):
                    row = slice(7, 8) if direction == 0 else slice(0, 1)
                    halo_o[number, field, row, :] = jnp.zeros((1, 128), jnp.float32)

        @pl.when(jnp.logical_not(has_x[1 - direction]))
        def _():
            for number in range(2 * STEPS):
                for place in range(4):
                    halo_x[number, direction, place] = none

    for stress in (stress_a, stress_b):
        for field in (YZ, XZ, ZZ):
            for z in (0, 1, layers + 2, layers + 3):
                stress[field, z] = none
    for speed in (speed_b, speed_c):
        for field in range(3):
            for z in (0, 1, layers + 2, layers + 3):
                speed[field, z] = none

    row_at = lax.broadcasted_iota(jnp.int32, tile, 0)
    lane_at = lax.broadcasted_iota(jnp.int32, tile, 1)
    group_at = lane_at // 4

    def rows_copy(number, source, direction, chunk):
        rows = pl.ds(6, 2) if direction == 0 else pl.ds(0, 2)
        return pltpu.make_async_remote_copy(
            source.at[pl.ds(0, 3), pl.ds(2 + chunk * CHUNK, CHUNK), rows, :],
            halo_y.at[number, :, pl.ds(chunk * CHUNK, CHUNK), rows, :],
            send_y.at[number, direction, chunk],
            recv_y.at[number, direction, chunk],
            device_id=to_y[direction],
        )

    def ocean_copy(number, direction):
        count = 2 if number % 2 == 0 else 1
        row = pl.ds(7, 1) if direction == 0 else pl.ds(0, 1)
        return pltpu.make_async_remote_copy(
            edges.at[number, pl.ds(0, count), row, :],
            halo_o.at[number, pl.ds(0, count), row, :],
            send_o.at[number, direction],
            recv_o.at[number, direction],
            device_id=to_y[direction],
        )

    def columns_copy(number, direction):
        return pltpu.make_async_remote_copy(
            pack.at[number],
            halo_x.at[number, direction],
            send_x.at[number, direction],
            recv_x.at[number, direction],
            device_id=to_x[direction],
        )

    def begin(make, has):
        for direction in range(2):

            @pl.when(has[direction])
            def _():
                make(direction).start()

    def arrive(make, has):
        for direction in range(2):

            @pl.when(has[1 - direction])
            def _():
                make(direction).wait_recv()

    def leave(make, has):
        for direction in range(2):

            @pl.when(has[direction])
            def _():
                make(direction).wait_send()

    def packed(held, tile_z, inner):
        return jnp.where(group_at == inner, turned(tile_z, 2 + 4 * inner, 1), held)

    def settle(held, part, chunk):
        moved = pltpu.roll(part, chunk * (4 * CHUNK), 1)
        return jnp.where(lane_at // (4 * CHUNK) == chunk, moved, held)

    def columns(number, place):
        low, high = halo_x[number, 0, place], halo_x[number, 1, place]
        return jnp.where(lane_at % 4 < 2, low, high)

    def chunk_columns(number, place, chunk):
        return pltpu.roll(columns(number, place), (128 - chunk * (4 * CHUNK)) % 128, 1)

    def unpacked(part, inner):
        return turned(part, -(2 + 4 * inner), 1)

    def shifted(tile_z, halo, axis, by):
        at, size = (row_at, 8) if axis == 0 else (lane_at, 128)
        from_halo = at >= size - by if by > 0 else at < -by
        return turned(jnp.where(from_halo, halo, tile_z), by, axis)

    def differ(tile_z, halo, axis, forward):
        before = shifted(tile_z, halo, axis, 1)
        after = shifted(tile_z, halo, axis, -1)
        if forward:
            after_two = shifted(tile_z, halo, axis, -2)
            return near * (after - tile_z) + far * (after_two - before)
        before_two = shifted(tile_z, halo, axis, 2)
        return near * (tile_z - before) + far * (after - before_two)

    def differ_z(ref, field, z, forward):
        at = [ref[field, z + 2 + k] for k in ((-1, 0, 1, 2) if forward else (-2, -1, 0, 1))]
        return near * (at[2] - at[1]) + far * (at[3] - at[0])

    def zero_pack():
        return (none, none, none)

    def pack_stress(stress, chunk, held):
        parts = [none, none, none]
        for inner in range(CHUNK):
            for place, field in enumerate((XX, XY, XZ)):
                parts[place] = packed(parts[place], stress[field, chunk * CHUNK + inner + 2], inner)
        return tuple(settle(h, p, chunk) for h, p in zip(held, parts))

    def finish_pack(number, held, extra):
        for place in range(3):
            pack[number, place] = held[place]
        last = none
        for place, item in enumerate(extra):
            last = packed(last, item, place)
        pack[number, 3] = last

    def velocity_stage(number, stress, speed_old, speed_new):
        arrive(functools.partial(columns_copy, number), has_x)

        def body(chunk, held):
            arrive(lambda d: rows_copy(number, stress, d, chunk), has_y)
            side = [chunk_columns(number, place, chunk) for place in range(3)]
            parts = [none, none, none]
            for inner in range(CHUNK):
                z = chunk * CHUNK + inner
                sxx, sxy, sxz = stress[XX, z + 2], stress[XY, z + 2], stress[XZ, z + 2]
                syy, syz = stress[YY, z + 2], stress[YZ, z + 2]
                hx = [unpacked(s, inner) for s in side]
                ax = (
                    differ(sxx, hx[0], 1, True)
                    + differ(sxy, halo_y[number, XY, z], 0, False)
                    + differ_z(stress, XZ, z, False)
                )
                ay = (
                    differ(sxy, hx[1], 1, False)
                    + differ(syy, halo_y[number, YY, z], 0, True)
                    + differ_z(stress, YZ, z, False)
                )
                az = (
                    differ(sxz, hx[2], 1, False)
                    + differ(syz, halo_y[number, YZ, z], 0, False)
                    + differ_z(stress, ZZ, z, True)
                )
                rate = courant * buoy[z]
                for field, push in enumerate((ax, ay, az)):
                    old = speed_old[field, z] if speed_old is speed_a else speed_old[field, z + 2]
                    new = old + rate * push
                    speed_new[field, z + 2] = new
                    if speed_new is speed_c:
                        wave_out[field, z] = new
                    parts[field] = packed(parts[field], new, inner)
            begin(lambda d: rows_copy(number + 1, speed_new, d, chunk), has_y)
            return tuple(settle(h, p, chunk) for h, p in zip(held, parts))

        return lax.fori_loop(0, chunks, body, zero_pack())

    def stress_stage(number, speed, stress_old, write, send):
        arrive(functools.partial(columns_copy, number), has_x)

        def body(chunk, held):
            arrive(lambda d: rows_copy(number, speed, d, chunk), has_y)
            side = [chunk_columns(number, place, chunk) for place in range(3)]
            parts = [none, none, none]
            for inner in range(CHUNK):
                z = chunk * CHUNK + inner
                vx, vy, vz = speed[0, z + 2], speed[1, z + 2], speed[2, z + 2]
                hx = [unpacked(s, inner) for s in side]
                hy = [halo_y[number, field, z] for field in range(3)]
                strain_x = differ(vx, hx[0], 1, False)
                strain_y = differ(vy, hy[1], 0, False)
                strain_z = differ_z(speed, 2, z, False)
                shear_xy = differ(vx, hy[0], 0, True) + differ(vy, hx[1], 1, True)
                shear_xz = differ_z(speed, 0, z, True) + differ(vz, hx[2], 1, True)
                shear_yz = differ_z(speed, 1, z, True) + differ(vz, hy[2], 0, True)
                rate = courant * shear[z]
                bulk = (courant * lame[z]) * (strain_x + strain_y + strain_z)
                twice = 2.0 * rate
                press = jnp.where(index[...] == z, edges[number, 2], 0.0)
                new = {
                    XX: stress_old[XX, z + 2] + (bulk + twice * strain_x),
                    YY: stress_old[YY, z + 2] + (bulk + twice * strain_y),
                    ZZ: stress_old[ZZ, z + 2] + (bulk + twice * strain_z) - press,
                    XY: stress_old[XY, z + 2] + rate * shear_xy,
                    XZ: stress_old[XZ, z + 2] + rate * shear_xz,
                    YZ: stress_old[YZ, z + 2] + rate * shear_yz,
                }
                write(new, z)
                if send:
                    for place, field in enumerate((XX, XY, XZ)):
                        parts[place] = packed(parts[place], new[field], inner)
            if send:
                begin(lambda d: rows_copy(number + 1, stress_b, d, chunk), has_y)
                return tuple(settle(h, p, chunk) for h, p in zip(held, parts))
            return held

        return lax.fori_loop(0, chunks, body, zero_pack())

    def centred(tile_o, halo, axis):
        return 0.5 * (shifted(tile_o, halo, axis, -1) - shifted(tile_o, halo, axis, 1))

    def around(tile_o, rows, cols):
        return (
            shifted(tile_o, cols, 1, -1)
            + shifted(tile_o, cols, 1, 1)
            + shifted(tile_o, rows, 0, -1)
            + shifted(tile_o, rows, 0, 1)
            - 4.0 * tile_o
        )

    def level_stage(number, speed, level, flux_x, flux_y):
        arrive(functools.partial(ocean_copy, number), has_y)
        side = columns(number, 3)
        rows_y = halo_o[number, 1]
        seafloor = none
        for z in range(layers // 2):
            seafloor = seafloor + jnp.where(index[...] == z, speed[2, z + 2], 0.0)
        spread = centred(flux_x, unpacked(side, 0), 1) + centred(flux_y, rows_y, 0)
        wet = wet_i[...].astype(jnp.float32)
        level = level + wet * (uplift * seafloor - ocean_rate * spread)
        edges[number + 1, 0] = level
        edges[number + 1, 2] = loading * (wet * level)
        begin(functools.partial(ocean_copy, number + 1), has_y)
        return level

    def flux_stage(number, level, flux_x, flux_y):
        arrive(functools.partial(ocean_copy, number + 1), has_y)
        side = columns(number, 3)
        level_side = unpacked(columns(number + 1, 3), 0)
        slope_x = centred(level, level_side, 1)
        slope_y = centred(level, halo_o[number + 1, 0], 0)
        wet = wet_i[...].astype(jnp.float32)
        around_x = around(flux_x, halo_o[number, 0], unpacked(side, 0))
        around_y = around(flux_y, halo_o[number, 1], unpacked(side, 1))
        pull = ocean_rate * depth[...]
        return (
            wet * (flux_x - pull * slope_x + viscous * around_x),
            wet * (flux_y - pull * slope_y + viscous * around_y),
        )

    def write_middle(new, z):
        for field, value in new.items():
            stress_b[field, z + 2] = value

    def write_last(new, z):
        for field, value in new.items():
            wave_out[STRESS_SOURCE[field], z] = value

    for copy in loads[:7]:
        copy.wait()
    level, flux_x, flux_y = ocean[0], ocean[1], ocean[2]
    held = lax.fori_loop(
        0, chunks, lambda chunk, held: pack_stress(stress_a, chunk, held), zero_pack()
    )
    finish_pack(0, held, (flux_x, flux_y))
    edges[0, 0] = flux_x
    edges[0, 1] = flux_y
    peers = sum(has.astype(jnp.int32) for has in (*has_y, *has_x))
    pl.semaphore_wait(barrier, peers)

    for chunk in range(chunks):
        begin(lambda d: rows_copy(0, stress_a, d, chunk), has_y)
    begin(functools.partial(columns_copy, 0), has_x)
    begin(functools.partial(ocean_copy, 0), has_y)
    for copy in loads[7:]:
        copy.wait()

    speeds = (speed_a, speed_b, speed_c)
    stresses = (stress_a, stress_b)
    for step in range(STEPS):
        number = 2 * step
        last = step == STEPS - 1
        held = velocity_stage(number, stresses[step], speeds[step], speeds[step + 1])
        new_level = level_stage(number, speeds[step + 1], level, flux_x, flux_y)
        finish_pack(number + 1, held, (new_level,))
        begin(functools.partial(columns_copy, number + 1), has_x)
        held = stress_stage(
            number + 1,
            speeds[step + 1],
            stresses[step],
            write_last if last else write_middle,
            not last,
        )
        flux_x, flux_y = flux_stage(number, new_level, flux_x, flux_y)
        level = new_level
        if not last:
            edges[number + 2, 0] = flux_x
            edges[number + 2, 1] = flux_y
            finish_pack(number + 2, held, (flux_x, flux_y))
            begin(functools.partial(columns_copy, number + 2), has_x)
            begin(functools.partial(ocean_copy, number + 2), has_y)

    ocean_out[0] = level
    ocean_out[1] = flux_x
    ocean_out[2] = flux_y

    sources = (stress_a, speed_b, stress_b, speed_c)
    for number in range(2 * STEPS):

        def drain(chunk, carry):
            leave(lambda d: rows_copy(number, sources[number], d, chunk), has_y)
            return carry

        lax.fori_loop(0, chunks, drain, 0)
        leave(functools.partial(ocean_copy, number), has_y)
        leave(functools.partial(columns_copy, number), has_x)


def hand_on(waves, sea, waves_out, sea_out, sem):
    copies = [
        pltpu.make_async_copy(waves, waves_out, sem.at[0]),
        pltpu.make_async_copy(sea, sea_out, sem.at[1]),
    ]
    for copy in copies:
        copy.start()
    for copy in copies:
        copy.wait()


def solution(mesh):
    counts = (mesh.shape["gx"], mesh.shape["gy"])

    def local(*arrays):
        fields, ocean = arrays[0], arrays[4]
        layers = fields.shape[1]
        chunks = layers // CHUNK
        f32, dma = jnp.float32, pltpu.SemaphoreType.DMA
        rounds = 2 * STEPS
        cube = (layers, 8, 128)
        padded = (layers + 4, 8, 128)
        waves, sea = pl.pallas_call(
            functools.partial(kernel, counts),
            out_shape=(
                pltpu.VMEM(fields.shape, f32),
                pltpu.VMEM(ocean.shape, f32),
            ),
            in_specs=[pl.BlockSpec(memory_space=pl.ANY)] * 8,
            out_specs=(pl.BlockSpec(memory_space=pltpu.VMEM), pl.BlockSpec(memory_space=pltpu.VMEM)),
            scratch_shapes=[
                pltpu.VMEM((6, *padded), f32),
                pltpu.VMEM((3, *cube), f32),
                pltpu.VMEM(cube, f32),
                pltpu.VMEM(cube, f32),
                pltpu.VMEM(cube, f32),
                pltpu.VMEM((3, 8, 128), f32),
                pltpu.VMEM((8, 128), f32),
                pltpu.VMEM((8, 128), jnp.int32),
                pltpu.VMEM((8, 128), jnp.int32),
                pltpu.VMEM((6, *padded), f32),
                pltpu.VMEM((3, *padded), f32),
                pltpu.VMEM((3, *padded), f32),
                pltpu.VMEM((rounds, 3, *cube), f32),
                pltpu.VMEM((rounds, 2, 8, 128), f32),
                pltpu.VMEM((rounds, 4, 8, 128), f32),
                pltpu.VMEM((rounds, 2, 4, 8, 128), f32),
                pltpu.VMEM((rounds, 3, 8, 128), f32),
                dma((14,)),
                dma((rounds, 2, chunks)),
                dma((rounds, 2, chunks)),
                dma((rounds, 2)),
                dma((rounds, 2)),
                dma((rounds, 2)),
                dma((rounds, 2)),
            ],
            compiler_params=pltpu.CompilerParams(collective_id=0, has_side_effects=True, vmem_limit_bytes=60 << 20),
            name="waves",
        )(*arrays)
        return pl.pallas_call(
            hand_on,
            out_shape=(
                jax.ShapeDtypeStruct(fields.shape, f32),
                jax.ShapeDtypeStruct(ocean.shape, f32),
            ),
            in_specs=[pl.BlockSpec(memory_space=pltpu.VMEM)] * 2,
            out_specs=(pl.BlockSpec(memory_space=pl.ANY), pl.BlockSpec(memory_space=pl.ANY)),
            scratch_shapes=[dma((2,))],
            compiler_params=pltpu.CompilerParams(vmem_limit_bytes=12 << 20),
            name="hand_on",
        )(waves, sea)

    flat = P("gy", "gx")
    deep = P(None, "gy", "gx")
    in_specs = (P(None, None, "gy", "gx"), deep, deep, deep, deep, flat, flat, flat)
    out_specs = (P(None, None, "gy", "gx"), deep)
    return jax.shard_map(local, mesh=mesh, in_specs=in_specs, out_specs=out_specs, check_vma=False)
```

```python
import functools

import jax
import jax.numpy as jnp
from jax import lax
from jax.experimental import pallas as pl
from jax.experimental.pallas import tpu as pltpu
from jax.sharding import PartitionSpec as P

STEPS = 2
CHUNK = 8
TILE = (8, 128)

near = 9.0 / 8.0
far = -1.0 / 24.0
courant = 0.3
ocean_rate = 0.3
uplift = 0.5
loading = 0.5
viscous = 0.1

XX, YY, ZZ, XY, XZ, YZ = range(6)
ALONG_X = ((XX, True), (XY, False), (XZ, False))
ALONG_Y = ((XY, False), (YY, True), (YZ, False))
FIELD = (0, 2, 1)
ALONG_Z = ((XZ, False), (YZ, False), (ZZ, True))


def turned(tile, shift, axis):
    return pltpu.roll(tile, shift % tile.shape[axis], axis)


def kernel(
    counts,
    fields_ref,
    lame_ref,
    shear_ref,
    buoy_ref,
    ocean_ref,
    depth_ref,
    index_ref,
    wet_ref,
    wave_out,
    ocean_out,
    stress_a,
    stress_b,
    speed_a,
    speed_b,
    speed_c,
    lame,
    shear,
    buoy,
    sea,
    depth,
    index,
    wet_i,
    press,
    pushed,
    wraps,
    packs,
    rows_o,
    packs_o,
    halo_wraps,
    halo_pushed,
    halo_buoy,
    halo_x,
    halo_d,
    halo_oy,
    halo_ox,
    halo_od,
    speed_rows,
    speed_cols,
    load_sem,
    send_y,
    recv_y,
    send_b,
    recv_b,
    send_x,
    recv_x,
    send_d,
    recv_d,
    send_oy,
    recv_oy,
    send_ox,
    recv_ox,
    send_od,
    recv_od,
):
    count_x, count_y = counts
    at_x, at_y = lax.axis_index("gx"), lax.axis_index("gy")
    layers = fields_ref.shape[1]
    chunks = layers // CHUNK

    next_x = (jnp.minimum(at_x + 1, count_x - 1), jnp.maximum(at_x - 1, 0))
    next_y = (jnp.minimum(at_y + 1, count_y - 1), jnp.maximum(at_y - 1, 0))
    inside_x = (at_x < count_x - 1, at_x > 0)
    inside_y = (at_y < count_y - 1, at_y > 0)
    to_y = tuple({"gy": y} for y in next_y)
    to_x = tuple({"gx": x} for x in next_x)
    to_d = tuple({"gx": next_x[d // 2], "gy": next_y[d % 2]} for d in range(4))
    inside_d = tuple(jnp.logical_and(inside_x[d // 2], inside_y[d % 2]) for d in range(4))

    def each(inside, act):
        for direction, there in enumerate(inside):
            pl.when(there)(functools.partial(act, direction))

    from_x = inside_x[::-1]
    from_y = inside_y[::-1]
    from_d = inside_d[::-1]

    barrier = pltpu.get_barrier_semaphore()
    for inside, to in ((inside_y, to_y), (inside_d, to_d), (inside_x, to_x)):
        each(
            inside,
            lambda d, to=to: pl.semaphore_signal(barrier, inc=1, device_id=to[d]),
        )

    loads = []

    def load(source, target):
        copy = pltpu.make_async_copy(source, target, load_sem.at[len(loads)])
        copy.start()
        loads.append(copy)

    inner_layers = pl.ds(2, layers)
    load(fields_ref.at[pl.ds(3, 6)], stress_a.at[:, inner_layers])
    load(fields_ref.at[pl.ds(0, 3)], speed_a.at[:, inner_layers])
    load(buoy_ref, buoy.at[pl.ds(0, layers)])
    load(ocean_ref, sea.at[0])
    load(depth_ref, depth)
    load(index_ref, index)
    load(wet_ref, wet_i)
    load(lame_ref, lame)
    load(shear_ref, shear)

    none = jnp.zeros(TILE, jnp.float32)
    row_at = lax.broadcasted_iota(jnp.int32, TILE, 0)
    lane_at = lax.broadcasted_iota(jnp.int32, TILE, 1)
    group_at = lane_at // 4
    slot_at = lane_at % 4
    low_slot = slot_at < 2
    upper = row_at < 4
    edge_rows = jnp.logical_or(row_at < 2, row_at >= 6)
    edge_lanes = jnp.logical_or(lane_at < 2, lane_at >= 126)
    wrap_back = jnp.logical_or(row_at < 2, row_at >= 7)
    wrap_ahead = jnp.logical_or(row_at < 1, row_at >= 6)
    wrap_rows = (wrap_back, wrap_ahead, wrap_back)

    margins = (0, 1, layers + 2, layers + 3)
    for z in margins:
        for field in (XZ, YZ, ZZ):
            stress_a[field, z] = none
            stress_b[field, z] = none
        for field in range(3):
            speed_b[field, z] = none
            speed_c[field, z] = none

    wrap_parts = ((pl.ds(0, 2), (pl.ds(0, 2), pl.ds(7, 1))), (pl.ds(2, 1), (pl.ds(0, 1), pl.ds(6, 2))))
    push_parts = ((pl.ds(0, 2), (pl.ds(7, 1), pl.ds(0, 2))), (pl.ds(2, 1), (pl.ds(6, 2), pl.ds(0, 1))))

    def layers_of(chunk):
        return pl.ds(0, layers) if chunk is None else pl.ds(chunk * CHUNK, CHUNK)

    def rows_copies(step, direction, chunk, which):
        source, target = ((wraps, halo_wraps), (pushed, halo_pushed))[which]
        result = []
        for part, (fields, rows) in enumerate((wrap_parts, push_parts)[which]):
            box = (step, fields, layers_of(chunk), rows[direction], slice(None))
            result.append(
                pltpu.make_async_remote_copy(
                    source.at[box],
                    target.at[box],
                    send_y.at[step, direction, which, part],
                    recv_y.at[step, direction, which, part, 0 if chunk is None else chunk],
                    device_id=to_y[direction],
                )
            )
        return result

    def buoy_copy(direction):
        rows = pl.ds(6, 2) if direction == 0 else pl.ds(0, 2)
        return pltpu.make_async_remote_copy(
            buoy_ref.at[:, rows, :],
            halo_buoy.at[:, rows, :],
            send_b.at[direction],
            recv_b.at[direction],
            device_id=to_y[direction],
        )

    def chunk_at(chunk):
        return pl.ds(0, chunks) if chunk is None else pl.ds(chunk, 1)

    def columns_copy(step, direction, chunk):
        return pltpu.make_async_remote_copy(
            packs.at[step, chunk_at(chunk), pl.ds(0, 2)],
            halo_x.at[step, direction, chunk_at(chunk)],
            send_x.at[step, direction],
            recv_x.at[step, direction, 0 if chunk is None else chunk],
            device_id=to_x[direction],
        )

    def corner_copy(step, corner, chunk):
        rows = pl.ds(4, 4) if corner % 2 == 0 else pl.ds(0, 4)
        return pltpu.make_async_remote_copy(
            packs.at[step, chunk_at(chunk), 2, rows, :],
            halo_d.at[step, corner, chunk_at(chunk), rows, :],
            send_d.at[step, corner],
            recv_d.at[step, corner, 0 if chunk is None else chunk],
            device_id=to_d[corner],
        )

    def ocean_rows(step, direction):
        row = pl.ds(7, 1) if direction == 0 else pl.ds(0, 1)
        return pltpu.make_async_remote_copy(
            rows_o.at[step, :, row, :],
            halo_oy.at[step, :, row, :],
            send_oy.at[step, direction],
            recv_oy.at[step, direction],
            device_id=to_y[direction],
        )

    def ocean_columns(step, direction):
        return pltpu.make_async_remote_copy(
            packs_o.at[step],
            halo_ox.at[step, direction],
            send_ox.at[step, direction],
            recv_ox.at[step, direction],
            device_id=to_x[direction],
        )

    def ocean_corner(step, corner):
        return pltpu.make_async_remote_copy(
            packs_o.at[step],
            halo_od.at[step, corner],
            send_od.at[step, corner],
            recv_od.at[step, corner],
            device_id=to_d[corner],
        )

    def start_chunk(step, chunk):
        def start_rows(direction):
            for which in range(2):
                for copy in rows_copies(step, direction, chunk, which):
                    copy.start()

        each(inside_y, start_rows)
        each(inside_d, lambda d: corner_copy(step, d, chunk).start())
        each(inside_x, lambda d: columns_copy(step, d, chunk).start())

    def start_ocean(step):
        each(inside_y, lambda d: ocean_rows(step, d).start())
        each(inside_d, lambda d: ocean_corner(step, d).start())
        each(inside_x, lambda d: ocean_columns(step, d).start())

    def wait_rows(step, chunk, which):
        def wait(direction):
            for copy in rows_copies(step, direction, chunk, which):
                copy.wait_recv()

        each(from_y, wait)

    def drain(step):
        def rows(direction):
            for which in range(2):
                for copy in rows_copies(step, direction, None, which):
                    copy.wait_send()
            ocean_rows(step, direction).wait_send()
            if step == 0:
                buoy_copy(direction).wait_send()

        def corner(d):
            corner_copy(step, d, None).wait_send()
            ocean_corner(step, d).wait_send()

        def columns(direction):
            columns_copy(step, direction, None).wait_send()
            ocean_columns(step, direction).wait_send()

        each(inside_y, rows)
        each(inside_d, corner)
        each(inside_x, columns)

    def clear_rows(direction):
        first = direction == 0
        push_rows = slice(6, 8) if first else slice(0, 2)
        wrap_rows = slice(0, 2) if first else slice(6, 8)
        zeros = jnp.zeros((2, 128), jnp.float32)

        def clear(z, carry):
            halo_buoy[z, push_rows, :] = zeros
            for step in range(STEPS):
                for field in range(3):
                    halo_pushed[step, field, z, push_rows, :] = zeros
                    halo_wraps[step, field, z, wrap_rows, :] = zeros
            return carry

        lax.fori_loop(0, layers, clear, 0)
        for step in range(STEPS):
            for item in range(5):
                halo_oy[step, item, push_rows, :] = zeros

    def clear_columns(direction):
        for step in range(STEPS):
            halo_ox[step, direction] = none
            for chunk in range(chunks):
                for part in range(2):
                    halo_x[step, direction, chunk, part] = none

    def clear_corner(corner):
        for step in range(STEPS):
            halo_od[step, corner] = none
            for chunk in range(chunks):
                halo_d[step, corner, chunk] = none

    each(tuple(jnp.logical_not(there) for there in from_y), clear_rows)
    each(tuple(jnp.logical_not(there) for there in from_x), clear_columns)
    each(tuple(jnp.logical_not(there) for there in from_d), clear_corner)

    def packed(held, tile, place):
        return jnp.where(group_at == place, turned(tile, 2 + 4 * place, 1), held)

    def unpacked(part, place):
        return turned(part, -(2 + 4 * place), 1)

    def shifted(tile, halo, axis, by):
        at, size = (row_at, 8) if axis == 0 else (lane_at, 128)
        from_halo = at >= size - by if by > 0 else at < -by
        return turned(jnp.where(from_halo, halo, tile), by, axis)

    def differ(tile, halo, axis, forward):
        before = shifted(tile, halo, axis, 1)
        after = shifted(tile, halo, axis, -1)
        if forward:
            after_two = shifted(tile, halo, axis, -2)
            return near * (after - tile) + far * (after_two - before)
        before_two = shifted(tile, halo, axis, 2)
        return near * (tile - before) + far * (after - before_two)

    def differ_z(ref, field, z, forward):
        at = [ref[field, z + 2 + k] for k in ((-1, 0, 1, 2) if forward else (-2, -1, 0, 1))]
        return near * (at[2] - at[1]) + far * (at[3] - at[0])

    def weight(mask, value):
        return jnp.where(mask, jnp.float32(value), jnp.float32(0.0))

    def wrapped(tile, axis, forward, low_one, low_two, high_one, high_two):
        before, after = turned(tile, 1, axis), turned(tile, -1, axis)
        if forward:
            return (
                weight(low_one, -far) * before
                + weight(high_one, near) * after
                + weight(high_two, far) * turned(tile, -2, axis)
            )
        return (
            weight(low_one, -near) * before
            + weight(low_two, -far) * turned(tile, 2, axis)
            + weight(high_one, far) * after
        )

    row_ends = (row_at < 1, row_at < 2, row_at >= 7, row_at >= 6)
    slot_ends = (slot_at == 2, slot_at >= 2, slot_at == 1, slot_at < 2)

    def circular_y(tile, forward):
        before, after = turned(tile, 1, 0), turned(tile, -1, 0)
        low_one, low_two, high_one, high_two = row_ends
        if forward:
            two = turned(tile, -2, 0)
            whole = near * (after - tile) + far * (two - before)
            wrap = (
                weight(low_one, -far) * before
                + weight(high_one, near) * after
                + weight(high_two, far) * two
            )
        else:
            two = turned(tile, 2, 0)
            whole = near * (tile - before) + far * (after - two)
            wrap = (
                weight(low_one, -near) * before
                + weight(low_two, -far) * two
                + weight(high_one, far) * after
            )
        return whole - wrap, wrap

    def local_x(tile, forward):
        before, after = turned(tile, 1, 1), turned(tile, -1, 1)
        if forward:
            two = turned(tile, -2, 1)
            return (
                weight(lane_at < 127, near) * after
                - near * tile
                + weight(lane_at < 126, far) * two
                - weight(lane_at >= 1, far) * before
            )
        two = turned(tile, 2, 1)
        return (
            near * tile
            - weight(lane_at >= 1, near) * before
            + weight(lane_at < 127, far) * after
            - weight(lane_at >= 2, far) * two
        )

    def push_chunk(step, chunk, stress, speed):
        edge_push, edge_x, edge_y = none, none, none
        for inner in range(CHUNK):
            z = chunk * CHUNK + inner
            rate = courant * buoy[z]
            edge_push = packed(edge_push, rate, 3 * CHUNK + inner)
            for axis in range(3):
                tile_x, tile_y = stress[ALONG_X[axis][0], z + 2], stress[ALONG_Y[axis][0], z + 2]
                kept, wrap = circular_y(tile_y, ALONG_Y[axis][1])
                total = (
                    local_x(tile_x, ALONG_X[axis][1])
                    + kept
                    + differ_z(stress, ALONG_Z[axis][0], z, ALONG_Z[axis][1])
                )
                push = speed[axis, z + 2] + rate * total
                pushed[step, FIELD[axis], z] = push
                wraps[step, FIELD[axis], z] = wrap
                place = axis * CHUNK + inner
                edge_push = packed(edge_push, push, place)
                edge_x = packed(edge_x, tile_x, place)
                edge_y = packed(edge_y, tile_y, place)
        first = lane_at < 4 * CHUNK
        second = jnp.logical_and(lane_at >= 4 * CHUNK, lane_at < 8 * CHUNK)
        packs[step, chunk, 0] = edge_push
        wrap_x = jnp.where(
            first, wrapped(edge_x, 1, True, *slot_ends), wrapped(edge_x, 1, False, *slot_ends)
        )
        packs[step, chunk, 1] = wrap_x
        wrap_y = jnp.where(
            second, wrapped(edge_y, 0, True, *row_ends), wrapped(edge_y, 0, False, *row_ends)
        )
        packs[step, chunk, 2] = jnp.where(edge_rows, wrap_x, turned(wrap_y, 4, 0))

    def join_chunk(step, chunk, speed):
        side = jnp.where(low_slot, halo_x[step, 1, chunk, 1], halo_x[step, 0, chunk, 1])
        for inner in range(CHUNK):
            z = chunk * CHUNK + inner
            rate = courant * buoy[z]
            for axis in range(3):
                added = jnp.where(wrap_rows[axis], halo_wraps[step, FIELD[axis], z], 0.0) + jnp.where(
                    edge_lanes, unpacked(side, axis * CHUNK + inner), 0.0
                )
                new = pushed[step, FIELD[axis], z] + rate * added
                speed[axis, z + 2] = new
                if step == STEPS - 1:
                    wave_out[axis, z] = new

    def corners(step, chunk):
        def of(dx):
            return jnp.where(
                upper, halo_d[step, 2 * dx + 1, chunk], halo_d[step, 2 * dx, chunk]
            )

        low, high = of(0), of(1)
        wrap_y = turned(jnp.where(low_slot, low, high), 4, 0)
        return jnp.where(low_slot, high, low), jnp.where(edge_rows, wrap_y, 0.0)

    def halo_chunk(step, chunk):
        wrap_x, wrap_y = corners(step, chunk)
        edge = jnp.where(low_slot, halo_x[step, 0, chunk, 0], halo_x[step, 1, chunk, 0])
        span = lane_at // (4 * CHUNK)
        rate_edge = jnp.where(
            span == 0,
            turned(edge, 4 * CHUNK, 1),
            jnp.where(span == 1, turned(edge, 8 * CHUNK, 1), turned(edge, 12 * CHUNK, 1)),
        )
        speed_cols[step, chunk] = edge + rate_edge * (packs[step, chunk, 1] + wrap_y)
        for inner in range(CHUNK):
            z = chunk * CHUNK + inner
            rate = courant * halo_buoy[z]
            for axis in range(3):
                added = wraps[step, FIELD[axis], z] + jnp.where(
                    edge_lanes, unpacked(wrap_x, axis * CHUNK + inner), 0.0
                )
                speed_rows[axis, z] = halo_pushed[step, FIELD[axis], z] + rate * added

    def stress_chunk(step, chunk, speed, stress_old, stress_new):
        side = speed_cols[step, chunk]
        for inner in range(CHUNK):
            z = chunk * CHUNK + inner
            vx, vy, vz = speed[0, z + 2], speed[1, z + 2], speed[2, z + 2]
            hx = [unpacked(side, axis * CHUNK + inner) for axis in range(3)]
            hy = [speed_rows[axis, z] for axis in range(3)]
            strain_x = differ(vx, hx[0], 1, False)
            strain_y = differ(vy, hy[1], 0, False)
            strain_z = differ_z(speed, 2, z, False)
            shear_xy = differ(vx, hy[0], 0, True) + differ(vy, hx[1], 1, True)
            shear_xz = differ_z(speed, 0, z, True) + differ(vz, hx[2], 1, True)
            shear_yz = differ_z(speed, 1, z, True) + differ(vz, hy[2], 0, True)
            rate = courant * shear[z]
            bulk = (courant * lame[z]) * (strain_x + strain_y + strain_z)
            twice = 2.0 * rate
            load_z = jnp.where(index[...] == z, press[step], 0.0)
            new = {
                XX: stress_old[XX, z + 2] + (bulk + twice * strain_x),
                YY: stress_old[YY, z + 2] + (bulk + twice * strain_y),
                ZZ: stress_old[ZZ, z + 2] + (bulk + twice * strain_z) - load_z,
                XY: stress_old[XY, z + 2] + rate * shear_xy,
                XZ: stress_old[XZ, z + 2] + rate * shear_xz,
                YZ: stress_old[YZ, z + 2] + rate * shear_yz,
            }
            for field, value in new.items():
                if step == STEPS - 1:
                    wave_out[3 + field, z] = value
                else:
                    stress_new[field, z + 2] = value

    def centred(tile, halo, axis):
        return 0.5 * (shifted(tile, halo, axis, -1) - shifted(tile, halo, axis, 1))

    def around(tile, rows, cols):
        return (
            shifted(tile, cols, 1, -1)
            + shifted(tile, cols, 1, 1)
            + shifted(tile, rows, 0, -1)
            + shifted(tile, rows, 0, 1)
            - 4.0 * tile
        )

    def ocean_prepare(step):
        level, flux_x, flux_y = sea[step, 0], sea[step, 1], sea[step, 2]
        wet = wet_i[...].astype(jnp.float32)
        spread = centred(flux_x, none, 1) + centred(flux_y, none, 0)
        items = (
            flux_x,
            flux_y,
            level - ocean_rate * (wet * spread),
            wet,
            index[...].astype(jnp.float32),
        )
        pack = none
        for place, item in enumerate(items):
            rows_o[step, place] = item
            pack = packed(pack, item, place)
        packs_o[step] = pack

    def ocean_edge(step):
        return jnp.where(low_slot, halo_ox[step, 0], halo_ox[step, 1])

    def ocean_level(step, speed):
        level, flux_x, flux_y = sea[step, 0], sea[step, 1], sea[step, 2]
        wet = wet_i[...].astype(jnp.float32)
        seafloor = none
        for z in range(layers // 2):
            seafloor = seafloor + jnp.where(index[...] == z, speed[2, z + 2], 0.0)
        spread = centred(flux_x, unpacked(ocean_edge(step), 0), 1) + centred(
            flux_y, halo_oy[step, 1], 0
        )
        level = level + wet * (uplift * seafloor - ocean_rate * spread)
        sea[step + 1, 0] = level
        press[step] = loading * (wet * level)

    def ocean_flux(step):
        level, flux_x, flux_y = sea[step + 1, 0], sea[step, 1], sea[step, 2]
        wet = wet_i[...].astype(jnp.float32)
        edge = ocean_edge(step)

        def of(dx):
            return jnp.where(upper, halo_od[step, 2 * dx + 1], halo_od[step, 2 * dx])

        corner = jnp.where(low_slot, of(0), of(1))

        index_rows = halo_oy[step, 4]
        seafloor = none
        for z in range(layers // 2):
            seafloor = seafloor + jnp.where(index_rows == z, speed_rows[2, z], 0.0)
        spread = centred(none, flux_y, 0) + centred(none, unpacked(corner, 0), 1)
        level_rows = halo_oy[step, 2] + halo_oy[step, 3] * (
            uplift * seafloor - ocean_rate * spread
        )

        own = packs_o[step]
        index_edge = jnp.where(lane_at < 4, turned(edge, -16, 1), 0.0)
        for by in (4, 8, 16):
            index_edge = index_edge + turned(index_edge, by, 1)
        index_edge = turned(index_edge, 8 * CHUNK, 1)
        total = none
        for chunk in range(layers // 2 // CHUNK):
            z_at = chunk * CHUNK + group_at - 2 * CHUNK
            chosen = jnp.logical_and(
                index_edge == z_at.astype(jnp.float32), lane_at // (4 * CHUNK) == 2
            )
            total = total + jnp.where(chosen, speed_cols[step, chunk], 0.0)
        total = turned(total, -8 * CHUNK, 1)
        for by in (16, 8, 4):
            total = total + turned(total, -by, 1)
        spread_edge = (
            jnp.where(slot_at == 1, 0.5 * turned(own, -1, 1), 0.0)
            - jnp.where(slot_at == 2, 0.5 * turned(own, 1, 1), 0.0)
            + centred(none, turned(corner, -4, 1), 0)
        )
        level_edge = turned(edge, -8, 1) + turned(edge, -12, 1) * (
            uplift * total - ocean_rate * spread_edge
        )

        slope_x = centred(level, unpacked(level_edge, 0), 1)
        slope_y = centred(level, level_rows, 0)
        around_x = around(flux_x, halo_oy[step, 0], unpacked(edge, 0))
        around_y = around(flux_y, halo_oy[step, 1], unpacked(edge, 1))
        pull = ocean_rate * depth[...]
        sea[step + 1, 1] = wet * (flux_x - pull * slope_x + viscous * around_x)
        sea[step + 1, 2] = wet * (flux_y - pull * slope_y + viscous * around_y)

    for copy in loads[:7]:
        copy.wait()
    speeds = (speed_a, speed_b, speed_c)
    stresses = (stress_a, stress_b, stress_b)

    def first_push(chunk, carry):
        push_chunk(0, chunk, stress_a, speed_a)
        return carry

    lax.fori_loop(0, chunks, first_push, 0)
    ocean_prepare(0)

    peers = sum(there.astype(jnp.int32) for there in (*inside_x, *inside_y, *inside_d))
    pl.semaphore_wait(barrier, peers)

    def first_send(chunk, carry):
        start_chunk(0, chunk)
        return carry

    start_chunk(0, 0)
    each(inside_y, lambda d: buoy_copy(d).start())
    start_ocean(0)
    lax.fori_loop(1, chunks, first_send, 0)
    for copy in loads[7:]:
        copy.wait()

    for step in range(STEPS):
        last = step == STEPS - 1
        speed_old, speed_new = speeds[step], speeds[step + 1]
        stress_old, stress_new = stresses[step], stresses[step + 1]

        def body(turn, carry):
            @pl.when(turn < chunks)
            def _():
                each(from_x, lambda d: columns_copy(step, d, turn).wait_recv())
                wait_rows(step, turn, 0)
                join_chunk(step, turn, speed_new)

            @pl.when(turn == 1)
            def _():
                each(from_x, lambda d: ocean_columns(step, d).wait_recv())
                each(from_y, lambda d: ocean_rows(step, d).wait_recv())
                ocean_level(step, speed_new)
                if step == 0:
                    each(from_y, lambda d: buoy_copy(d).wait_recv())

            @pl.when(jnp.logical_and(turn >= 1, turn <= chunks))
            def _():
                wait_rows(step, turn - 1, 1)
                each(from_d, lambda d: corner_copy(step, d, turn - 1).wait_recv())
                halo_chunk(step, turn - 1)
                stress_chunk(step, turn - 1, speed_new, stress_old, stress_new)

            @pl.when(turn == 2)
            def _():
                each(from_d, lambda d: ocean_corner(step, d).wait_recv())
                ocean_flux(step)
                if not last:
                    ocean_prepare(step + 1)
                    start_ocean(step + 1)

            if not last:

                @pl.when(turn >= 2)
                def _():
                    push_chunk(step + 1, turn - 2, stress_new, speed_new)
                    start_chunk(step + 1, turn - 2)

            return carry

        lax.fori_loop(0, chunks + (1 if last else 2), body, 0)
        drain(step)

    for item in range(3):
        ocean_out[item] = sea[STEPS, item]


def hand_on(waves, sea, waves_out, sea_out, sem):
    copies = [
        pltpu.make_async_copy(waves, waves_out, sem.at[0]),
        pltpu.make_async_copy(sea, sea_out, sem.at[1]),
    ]
    for copy in copies:
        copy.start()
    for copy in copies:
        copy.wait()


def solution(mesh):
    counts = (mesh.shape["gx"], mesh.shape["gy"])

    def local(*arrays):
        fields, ocean = arrays[0], arrays[4]
        layers = fields.shape[1]
        chunks = layers // CHUNK
        f32, dma = jnp.float32, pltpu.SemaphoreType.DMA
        cube = (layers, *TILE)
        padded = (layers + 4, *TILE)
        waves, sea = pl.pallas_call(
            functools.partial(kernel, counts),
            out_shape=(pltpu.VMEM(fields.shape, f32), pltpu.VMEM(ocean.shape, f32)),
            in_specs=[pl.BlockSpec(memory_space=pl.ANY)] * 8,
            out_specs=(
                pl.BlockSpec(memory_space=pltpu.VMEM),
                pl.BlockSpec(memory_space=pltpu.VMEM),
            ),
            scratch_shapes=[
                pltpu.VMEM((6, *padded), f32),
                pltpu.VMEM((6, *padded), f32),
                pltpu.VMEM((3, *padded), f32),
                pltpu.VMEM((3, *padded), f32),
                pltpu.VMEM((3, *padded), f32),
                pltpu.VMEM(cube, f32),
                pltpu.VMEM(cube, f32),
                pltpu.VMEM(cube, f32),
                pltpu.VMEM((STEPS + 1, 3, *TILE), f32),
                pltpu.VMEM(TILE, f32),
                pltpu.VMEM(TILE, jnp.int32),
                pltpu.VMEM(TILE, jnp.int32),
                pltpu.VMEM((STEPS, *TILE), f32),
                pltpu.VMEM((STEPS, 3, *cube), f32),
                pltpu.VMEM((STEPS, 3, *cube), f32),
                pltpu.VMEM((STEPS, chunks, 3, *TILE), f32),
                pltpu.VMEM((STEPS, 5, *TILE), f32),
                pltpu.VMEM((STEPS, *TILE), f32),
                pltpu.VMEM((STEPS, 3, *cube), f32),
                pltpu.VMEM((STEPS, 3, *cube), f32),
                pltpu.VMEM(cube, f32),
                pltpu.VMEM((STEPS, 2, chunks, 2, *TILE), f32),
                pltpu.VMEM((STEPS, 4, chunks, *TILE), f32),
                pltpu.VMEM((STEPS, 5, *TILE), f32),
                pltpu.VMEM((STEPS, 2, *TILE), f32),
                pltpu.VMEM((STEPS, 4, *TILE), f32),
                pltpu.VMEM((3, *cube), f32),
                pltpu.VMEM((STEPS, chunks, *TILE), f32),
                dma((9,)),
                dma((STEPS, 2, 2, 2)),
                dma((STEPS, 2, 2, 2, chunks)),
                dma((2,)),
                dma((2,)),
                dma((STEPS, 2)),
                dma((STEPS, 2, chunks)),
                dma((STEPS, 4)),
                dma((STEPS, 4, chunks)),
                dma((STEPS, 2)),
                dma((STEPS, 2)),
                dma((STEPS, 2)),
                dma((STEPS, 2)),
                dma((STEPS, 4)),
                dma((STEPS, 4)),
            ],
            compiler_params=pltpu.CompilerParams(
                collective_id=0, has_side_effects=True, vmem_limit_bytes=60 << 20
            ),
            name="waves",
        )(*arrays)
        return pl.pallas_call(
            hand_on,
            out_shape=(
                jax.ShapeDtypeStruct(fields.shape, f32),
                jax.ShapeDtypeStruct(ocean.shape, f32),
            ),
            in_specs=[pl.BlockSpec(memory_space=pltpu.VMEM)] * 2,
            out_specs=(pl.BlockSpec(memory_space=pl.ANY), pl.BlockSpec(memory_space=pl.ANY)),
            scratch_shapes=[dma((2,))],
            compiler_params=pltpu.CompilerParams(vmem_limit_bytes=12 << 20),
            name="hand_on",
        )(waves, sea)

    flat = P("gy", "gx")
    deep = P(None, "gy", "gx")
    in_specs = (P(None, None, "gy", "gx"), deep, deep, deep, deep, flat, flat, flat)
    out_specs = (P(None, None, "gy", "gx"), deep)
    return jax.shard_map(local, mesh=mesh, in_specs=in_specs, out_specs=out_specs, check_vma=False)
```

```python
import functools

import jax
import jax.numpy as jnp
from jax import lax
from jax.experimental import pallas as pl
from jax.experimental.pallas import tpu as pltpu
from jax.sharding import PartitionSpec as P

STEPS = 2
CHUNK = 8
TILE = (8, 128)

near = 9.0 / 8.0
far = -1.0 / 24.0
courant = 0.3
ocean_rate = 0.3
uplift = 0.5
loading = 0.5
viscous = 0.1

XX, YY, ZZ, XY, XZ, YZ = range(6)
ALONG_X = ((XX, True), (XY, False), (XZ, False))
ALONG_Y = ((XY, False), (YY, True), (YZ, False))
FIELD = (0, 2, 1)
ALONG_Z = ((XZ, False), (YZ, False), (ZZ, True))


def turned(tile, shift, axis):
    return pltpu.roll(tile, shift % tile.shape[axis], axis)


def kernel(
    counts,
    fields_ref,
    lame_ref,
    shear_ref,
    buoy_ref,
    ocean_ref,
    depth_ref,
    index_ref,
    wet_ref,
    wave_out,
    ocean_out,
    given,
    stress_b,
    speed_b,
    speed_c,
    lame,
    shear,
    buoy,
    sea,
    depth,
    index,
    wet_i,
    press,
    pushed,
    wraps,
    packs,
    rows_o,
    packs_o,
    halo_wraps,
    halo_pushed,
    halo_buoy,
    halo_x,
    halo_d,
    halo_oy,
    halo_ox,
    halo_od,
    speed_rows,
    speed_cols,
    cols_o,
    seafloor,
    sized,
    load_sem,
    send_y,
    recv_y,
    send_x,
    recv_x,
    send_d,
    recv_d,
):
    count_x, count_y = counts
    at_x, at_y = lax.axis_index("gx"), lax.axis_index("gy")
    layers = fields_ref.shape[1]
    chunks = layers // CHUNK

    next_x = (jnp.minimum(at_x + 1, count_x - 1), jnp.maximum(at_x - 1, 0))
    next_y = (jnp.minimum(at_y + 1, count_y - 1), jnp.maximum(at_y - 1, 0))
    inside_x = (at_x < count_x - 1, at_x > 0)
    inside_y = (at_y < count_y - 1, at_y > 0)
    to_y = tuple({"gy": y} for y in next_y)
    to_x = tuple({"gx": x} for x in next_x)
    to_d = tuple({"gx": next_x[d // 2], "gy": next_y[d % 2]} for d in range(4))
    inside_d = tuple(jnp.logical_and(inside_x[d // 2], inside_y[d % 2]) for d in range(4))

    def each(inside, act):
        for direction, there in enumerate(inside):
            pl.when(there)(functools.partial(act, direction))

    def when(condition, act):
        if isinstance(condition, bool):
            if condition:
                act()
        else:
            pl.when(condition)(act)

    from_x = inside_x[::-1]
    from_y = inside_y[::-1]
    from_d = inside_d[::-1]

    barrier = pltpu.get_barrier_semaphore()
    for inside, to in ((inside_y, to_y), (inside_d, to_d), (inside_x, to_x)):
        each(
            inside,
            lambda d, to=to: pl.semaphore_signal(barrier, inc=1, device_id=to[d]),
        )

    def rows_done(count, semaphore):
        part = sized.at[pl.ds(0, count)]
        pltpu.make_async_copy(part, part, semaphore).wait()

    inner_layers = pl.ds(2, layers)
    for source, target, place in (
        (fields_ref, given.at[:, inner_layers], 0),
        (buoy_ref, buoy, 1),
        (ocean_ref, sea.at[0], 2),
        (depth_ref, depth, 2),
        (index_ref, index, 2),
        (wet_ref, wet_i, 2),
        (lame_ref, lame, 3),
        (shear_ref, shear, 3),
    ):
        pltpu.make_async_copy(source, target, load_sem.at[place]).start()
    stress_a, speed_a = given.at[pl.ds(3, 6)], given.at[pl.ds(0, 3)]

    none = jnp.zeros(TILE, jnp.float32)
    row_at = lax.broadcasted_iota(jnp.int32, TILE, 0)
    lane_at = lax.broadcasted_iota(jnp.int32, TILE, 1)
    group_at = lane_at // 4
    slot_at = lane_at % 4
    low_slot = slot_at < 2
    upper = row_at < 4
    edge_rows = jnp.logical_or(row_at < 2, row_at >= 6)
    edge_lanes = jnp.logical_or(lane_at < 2, lane_at >= 126)
    wrap_back = jnp.logical_or(row_at < 2, row_at >= 7)
    wrap_ahead = jnp.logical_or(row_at < 1, row_at >= 6)
    wrap_rows = (wrap_back, wrap_ahead, wrap_back)

    for step in range(STEPS):
        for item in range(3):
            seafloor[step, item] = none
    margins = (0, 1, layers + 2, layers + 3)
    for z in margins:
        for field in (XZ, YZ, ZZ):
            stress_a[field, z] = none
            stress_b[field, z] = none
        for field in range(3):
            speed_b[field, z] = none
            speed_c[field, z] = none

    wrap_parts = ((pl.ds(0, 2), (pl.ds(0, 2), pl.ds(7, 1))), (pl.ds(2, 1), (pl.ds(0, 1), pl.ds(6, 2))))
    push_parts = ((pl.ds(0, 2), (pl.ds(7, 1), pl.ds(0, 2))), (pl.ds(2, 1), (pl.ds(6, 2), pl.ds(0, 1))))

    def rows_copies(step, direction, chunk):
        result = []
        span = pl.ds(chunk * CHUNK, CHUNK)

        def add(source, target):
            result.append(
                pltpu.make_async_remote_copy(
                    source,
                    target,
                    send_y.at[direction],
                    recv_y.at[step, direction, chunk],
                    device_id=to_y[direction],
                )
            )

        for source, target, parts in (
            (wraps, halo_wraps, wrap_parts),
            (pushed, halo_pushed, push_parts),
        ):
            for fields, rows in parts:
                box = (step, fields, span, rows[direction], slice(None))
                add(source.at[box], target.at[box])
        if step == 0:
            box = (span, pl.ds(6, 2) if direction == 0 else pl.ds(0, 2), slice(None))
            add(buoy_ref.at[box], halo_buoy.at[box])
        return result

    def rows_arrive(step, chunk):
        count = (11 if step == 0 else 9) * CHUNK + (5 if isinstance(chunk, int) and chunk == 1 else 0)
        each(from_y, lambda d: rows_done(count, recv_y.at[step, d, chunk]))

    def columns_arrive(step, half):
        count = 32 + (8 if half == 0 else 0)
        each(from_x, lambda d: rows_done(count, recv_x.at[step, d, half]))

    def corners_arrive(step, half):
        count = 8 + (8 if half == 0 else 0)
        each(from_d, lambda d: rows_done(count, recv_d.at[step, d, half]))

    def columns_copy(step, direction, half):
        return pltpu.make_async_remote_copy(
            packs.at[step, pl.ds(2 * half, 2), pl.ds(0, 2)],
            halo_x.at[step, direction, pl.ds(2 * half, 2)],
            send_x.at[direction],
            recv_x.at[step, direction, half],
            device_id=to_x[direction],
        )

    def corner_copy(step, corner, half):
        rows = pl.ds(4, 4) if corner % 2 == 0 else pl.ds(0, 4)
        return pltpu.make_async_remote_copy(
            packs.at[step, pl.ds(2 * half, 2), 2, rows, :],
            halo_d.at[step, corner, pl.ds(2 * half, 2), rows, :],
            send_d.at[corner],
            recv_d.at[step, corner, half],
            device_id=to_d[corner],
        )

    def ocean_rows(step, direction):
        row = pl.ds(7, 1) if direction == 0 else pl.ds(0, 1)
        return pltpu.make_async_remote_copy(
            rows_o.at[step, :, row, :],
            halo_oy.at[step, :, row, :],
            send_y.at[direction],
            recv_y.at[step, direction, 1],
            device_id=to_y[direction],
        )

    def ocean_columns(step, direction):
        return pltpu.make_async_remote_copy(
            packs_o.at[step],
            halo_ox.at[step, direction],
            send_x.at[direction],
            recv_x.at[step, direction, 0],
            device_id=to_x[direction],
        )

    def ocean_corner(step, corner):
        return pltpu.make_async_remote_copy(
            packs_o.at[step],
            halo_od.at[step, corner],
            send_d.at[corner],
            recv_d.at[step, corner, 0],
            device_id=to_d[corner],
        )

    def start_chunk(step, chunk):
        first = chunk == 1

        def start_rows(direction):
            for copy in rows_copies(step, direction, chunk):
                copy.start()
            when(first, lambda: ocean_rows(step, direction).start())

        each(inside_y, start_rows)

        def start_half():
            half = chunk // 2 if isinstance(chunk, int) else lax.div(chunk, 2)

            def start_corner(corner):
                corner_copy(step, corner, half).start()
                when(first, lambda: ocean_corner(step, corner).start())

            def start_columns(direction):
                columns_copy(step, direction, half).start()
                when(first, lambda: ocean_columns(step, direction).start())

            each(inside_d, start_corner)
            each(inside_x, start_columns)

        when(chunk % 2 == 1 if isinstance(chunk, int) else lax.rem(chunk, 2) == 1, start_half)

    def drain():
        rows_y = STEPS * (9 * layers + 5) + 2 * layers
        rows_x = STEPS * (2 * chunks + 1) * 8
        rows_d = STEPS * (4 * chunks + 8)
        each(inside_y, lambda d: rows_done(rows_y, send_y.at[d]))
        each(inside_d, lambda d: rows_done(rows_d, send_d.at[d]))
        each(inside_x, lambda d: rows_done(rows_x, send_x.at[d]))

    def clear_rows(direction):
        first = direction == 0
        push_rows = slice(6, 8) if first else slice(0, 2)
        wrap_rows = slice(0, 2) if first else slice(6, 8)
        zeros = jnp.zeros((2, 128), jnp.float32)

        def clear(z, carry):
            halo_buoy[z, push_rows, :] = zeros
            for step in range(STEPS):
                for field in range(3):
                    halo_pushed[step, field, z, push_rows, :] = zeros
                    halo_wraps[step, field, z, wrap_rows, :] = zeros
            return carry

        lax.fori_loop(0, layers, clear, 0)
        for step in range(STEPS):
            for item in range(5):
                halo_oy[step, item, push_rows, :] = zeros

    def clear_columns(direction):
        for step in range(STEPS):
            halo_ox[step, direction] = none
            for chunk in range(chunks):
                for part in range(2):
                    halo_x[step, direction, chunk, part] = none

    def clear_corner(corner):
        for step in range(STEPS):
            halo_od[step, corner] = none
            for chunk in range(chunks):
                halo_d[step, corner, chunk] = none

    each(tuple(jnp.logical_not(there) for there in from_y), clear_rows)
    each(tuple(jnp.logical_not(there) for there in from_x), clear_columns)
    each(tuple(jnp.logical_not(there) for there in from_d), clear_corner)

    def packed(held, tile, place):
        return jnp.where(group_at == place, turned(tile, 2 + 4 * place, 1), held)

    def unpacked(part, place):
        return turned(part, -(2 + 4 * place), 1)

    def shifted(tile, halo, axis, by):
        at, size = (row_at, 8) if axis == 0 else (lane_at, 128)
        from_halo = at >= size - by if by > 0 else at < -by
        return turned(jnp.where(from_halo, halo, tile), by, axis)

    def differ(tile, halo, axis, forward):
        before = shifted(tile, halo, axis, 1)
        after = shifted(tile, halo, axis, -1)
        if forward:
            after_two = shifted(tile, halo, axis, -2)
            return near * (after - tile) + far * (after_two - before)
        before_two = shifted(tile, halo, axis, 2)
        return near * (tile - before) + far * (after - before_two)

    def differ_z(ref, field, z, forward):
        at = [ref[field, z + 2 + k] for k in ((-1, 0, 1, 2) if forward else (-2, -1, 0, 1))]
        return near * (at[2] - at[1]) + far * (at[3] - at[0])

    def weight(mask, value):
        return jnp.where(mask, jnp.float32(value), jnp.float32(0.0))

    def wrapped(tile, axis, forward, low_one, low_two, high_one, high_two):
        before, after = turned(tile, 1, axis), turned(tile, -1, axis)
        if forward:
            return (
                weight(low_one, -far) * before
                + weight(high_one, near) * after
                + weight(high_two, far) * turned(tile, -2, axis)
            )
        return (
            weight(low_one, -near) * before
            + weight(low_two, -far) * turned(tile, 2, axis)
            + weight(high_one, far) * after
        )

    row_ends = (row_at < 1, row_at < 2, row_at >= 7, row_at >= 6)
    slot_ends = (slot_at == 2, slot_at >= 2, slot_at == 1, slot_at < 2)

    def circular_y(tile, forward):
        before, after = turned(tile, 1, 0), turned(tile, -1, 0)
        low_one, low_two, high_one, high_two = row_ends
        if forward:
            two = turned(tile, -2, 0)
            whole = near * (after - tile) + far * (two - before)
            wrap = (
                weight(low_one, -far) * before
                + weight(high_one, near) * after
                + weight(high_two, far) * two
            )
        else:
            two = turned(tile, 2, 0)
            whole = near * (tile - before) + far * (after - two)
            wrap = (
                weight(low_one, -near) * before
                + weight(low_two, -far) * two
                + weight(high_one, far) * after
            )
        return whole - wrap, wrap

    def local_x(tile, forward):
        before, after = turned(tile, 1, 1), turned(tile, -1, 1)
        if forward:
            two = turned(tile, -2, 1)
            return (
                weight(lane_at < 127, near) * after
                - near * tile
                + weight(lane_at < 126, far) * two
                - weight(lane_at >= 1, far) * before
            )
        two = turned(tile, 2, 1)
        return (
            near * tile
            - weight(lane_at >= 1, near) * before
            + weight(lane_at < 127, far) * after
            - weight(lane_at >= 2, far) * two
        )

    def push_chunk(step, chunk, stress, speed):
        edge_push = none if step == 0 else packs[0, chunk, 0]
        edge_x, edge_y = none, none
        for inner in range(CHUNK):
            z = chunk * CHUNK + inner
            rate = courant * buoy[z]
            if step == 0:
                edge_push = packed(edge_push, rate, 3 * CHUNK + inner)
            for axis in range(3):
                tile_x, tile_y = stress[ALONG_X[axis][0], z + 2], stress[ALONG_Y[axis][0], z + 2]
                kept, wrap = circular_y(tile_y, ALONG_Y[axis][1])
                total = (
                    local_x(tile_x, ALONG_X[axis][1])
                    + kept
                    + differ_z(stress, ALONG_Z[axis][0], z, ALONG_Z[axis][1])
                )
                push = speed[axis, z + 2] + rate * total
                pushed[step, FIELD[axis], z] = push
                wraps[step, FIELD[axis], z] = wrap
                place = axis * CHUNK + inner
                edge_push = packed(edge_push, push, place)
                edge_x = packed(edge_x, tile_x, place)
                edge_y = packed(edge_y, tile_y, place)
        first = lane_at < 4 * CHUNK
        second = jnp.logical_and(lane_at >= 4 * CHUNK, lane_at < 8 * CHUNK)
        packs[step, chunk, 0] = edge_push
        wrap_x = jnp.where(
            first, wrapped(edge_x, 1, True, *slot_ends), wrapped(edge_x, 1, False, *slot_ends)
        )
        packs[step, chunk, 1] = wrap_x
        wrap_y = jnp.where(
            second, wrapped(edge_y, 0, True, *row_ends), wrapped(edge_y, 0, False, *row_ends)
        )
        packs[step, chunk, 2] = jnp.where(edge_rows, wrap_x, turned(wrap_y, 4, 0))

    def join_chunk(step, chunk, speed):
        floor = none
        side = jnp.where(low_slot, halo_x[step, 1, chunk, 1], halo_x[step, 0, chunk, 1])
        for inner in range(CHUNK):
            z = chunk * CHUNK + inner
            rate = courant * buoy[z]
            for axis in range(3):
                added = jnp.where(wrap_rows[axis], halo_wraps[step, FIELD[axis], z], 0.0) + jnp.where(
                    edge_lanes, unpacked(side, axis * CHUNK + inner), 0.0
                )
                new = pushed[step, FIELD[axis], z] + rate * added
                speed[axis, z + 2] = new
                if axis == 2:
                    floor = floor + jnp.where(index[...] == z, new, 0.0)
                if step == STEPS - 1:
                    wave_out[axis, z] = new
        seafloor[step, 0] = seafloor[step, 0] + floor

    def corners(step, chunk):
        def of(dx):
            return jnp.where(
                upper, halo_d[step, 2 * dx + 1, chunk], halo_d[step, 2 * dx, chunk]
            )

        low, high = of(0), of(1)
        wrap_y = turned(jnp.where(low_slot, low, high), 4, 0)
        return jnp.where(low_slot, high, low), jnp.where(edge_rows, wrap_y, 0.0)

    def halo_chunk(step, chunk):
        wrap_x, wrap_y = corners(step, chunk)
        edge = jnp.where(low_slot, halo_x[step, 0, chunk, 0], halo_x[step, 1, chunk, 0])
        span = lane_at // (4 * CHUNK)
        rate_edge = jnp.where(
            span == 0,
            turned(edge, 4 * CHUNK, 1),
            jnp.where(span == 1, turned(edge, 8 * CHUNK, 1), turned(edge, 12 * CHUNK, 1)),
        )
        speed_cols[step, chunk] = edge + rate_edge * (packs[step, chunk, 1] + wrap_y)
        for inner in range(CHUNK):
            z = chunk * CHUNK + inner
            rate = courant * halo_buoy[z]
            for axis in range(3):
                added = wraps[step, FIELD[axis], z] + jnp.where(
                    edge_lanes, unpacked(wrap_x, axis * CHUNK + inner), 0.0
                )
                speed_rows[axis, z] = halo_pushed[step, FIELD[axis], z] + rate * added

    def stress_chunk(step, chunk, speed, stress_old, stress_new):
        side = speed_cols[step, chunk]
        floor_rows, floor_cols = none, none
        for inner in range(CHUNK):
            z = chunk * CHUNK + inner
            vx, vy, vz = speed[0, z + 2], speed[1, z + 2], speed[2, z + 2]
            hx = [unpacked(side, axis * CHUNK + inner) for axis in range(3)]
            hy = [speed_rows[axis, z] for axis in range(3)]
            floor_rows = floor_rows + jnp.where(halo_oy[step, 4] == z, hy[2], 0.0)
            floor_cols = floor_cols + jnp.where(cols_o[step, 4] == z, hx[2], 0.0)
            strain_x = differ(vx, hx[0], 1, False)
            strain_y = differ(vy, hy[1], 0, False)
            strain_z = differ_z(speed, 2, z, False)
            shear_xy = differ(vx, hy[0], 0, True) + differ(vy, hx[1], 1, True)
            shear_xz = differ_z(speed, 0, z, True) + differ(vz, hx[2], 1, True)
            shear_yz = differ_z(speed, 1, z, True) + differ(vz, hy[2], 0, True)
            rate = courant * shear[z]
            bulk = (courant * lame[z]) * (strain_x + strain_y + strain_z)
            twice = 2.0 * rate
            load_z = jnp.where(index[...] == z, press[step], 0.0)
            new = {
                XX: stress_old[XX, z + 2] + (bulk + twice * strain_x),
                YY: stress_old[YY, z + 2] + (bulk + twice * strain_y),
                ZZ: stress_old[ZZ, z + 2] + (bulk + twice * strain_z) - load_z,
                XY: stress_old[XY, z + 2] + rate * shear_xy,
                XZ: stress_old[XZ, z + 2] + rate * shear_xz,
                YZ: stress_old[YZ, z + 2] + rate * shear_yz,
            }
            for field, value in new.items():
                if step == STEPS - 1:
                    wave_out[3 + field, z] = value
                else:
                    stress_new[field, z + 2] = value
        seafloor[step, 1] = seafloor[step, 1] + floor_rows
        seafloor[step, 2] = seafloor[step, 2] + floor_cols

    def centred(tile, halo, axis):
        return 0.5 * (shifted(tile, halo, axis, -1) - shifted(tile, halo, axis, 1))

    def around(tile, rows, cols):
        return (
            shifted(tile, cols, 1, -1)
            + shifted(tile, cols, 1, 1)
            + shifted(tile, rows, 0, -1)
            + shifted(tile, rows, 0, 1)
            - 4.0 * tile
        )

    def ocean_prepare(step):
        level, flux_x, flux_y = sea[step, 0], sea[step, 1], sea[step, 2]
        wet = wet_i[...].astype(jnp.float32)
        spread = centred(flux_x, none, 1) + centred(flux_y, none, 0)
        items = (
            flux_x,
            flux_y,
            level - ocean_rate * (wet * spread),
            wet,
            index[...].astype(jnp.float32),
        )
        pack = none
        for place, item in enumerate(items):
            rows_o[step, place] = item
            pack = packed(pack, item, place)
        packs_o[step] = pack

    def ocean_level(step):
        level, flux_x, flux_y = sea[step, 0], sea[step, 1], sea[step, 2]
        wet = wet_i[...].astype(jnp.float32)
        edge = jnp.where(low_slot, halo_ox[step, 0], halo_ox[step, 1])
        cols = [unpacked(edge, item) for item in range(5)]
        for item in range(5):
            cols_o[step, item] = cols[item]
        spread = centred(flux_x, cols[0], 1) + centred(flux_y, halo_oy[step, 1], 0)
        level = level + wet * (uplift * seafloor[step, 0] - ocean_rate * spread)
        sea[step + 1, 0] = level
        press[step] = loading * (wet * level)

    def ocean_flux(step):
        level, flux_x, flux_y = sea[step + 1, 0], sea[step, 1], sea[step, 2]
        wet = wet_i[...].astype(jnp.float32)

        def of(dx):
            return jnp.where(upper, halo_od[step, 2 * dx + 1], halo_od[step, 2 * dx])

        corner = jnp.where(low_slot, of(0), of(1))

        spread = centred(none, flux_y, 0) + centred(none, unpacked(corner, 0), 1)
        level_rows = halo_oy[step, 2] + halo_oy[step, 3] * (
            uplift * seafloor[step, 1] - ocean_rate * spread
        )
        spread = centred(none, flux_x, 1) + centred(none, unpacked(corner, 1), 0)
        level_cols = cols_o[step, 2] + cols_o[step, 3] * (
            uplift * seafloor[step, 2] - ocean_rate * spread
        )
        slope_x = centred(level, level_cols, 1)
        slope_y = centred(level, level_rows, 0)
        around_x = around(flux_x, halo_oy[step, 0], cols_o[step, 0])
        around_y = around(flux_y, halo_oy[step, 1], cols_o[step, 1])
        pull = ocean_rate * depth[...]
        sea[step + 1, 1] = wet * (flux_x - pull * slope_x + viscous * around_x)
        sea[step + 1, 2] = wet * (flux_y - pull * slope_y + viscous * around_y)

    for count, place in ((9 * 8 * layers, 0), (8 * layers, 1), (6 * 8, 2)):
        rows_done(count, load_sem.at[place])
    speeds = (speed_a, speed_b, speed_c)
    stresses = (stress_a, stress_b, stress_b)

    def first_push(chunk, carry):
        push_chunk(0, chunk, stress_a, speed_a)
        return carry

    lax.fori_loop(0, 2, first_push, 0)
    ocean_prepare(0)

    peers = sum(there.astype(jnp.int32) for there in (*inside_x, *inside_y, *inside_d))
    pl.semaphore_wait(barrier, peers)

    def paced(chunk, carry):
        start_chunk(0, chunk - 2)
        push_chunk(0, chunk, stress_a, speed_a)
        return carry

    def first_send(chunk, carry):
        start_chunk(0, chunk)
        return carry

    lax.fori_loop(2, chunks, paced, 0)
    lax.fori_loop(chunks - 2, chunks, first_send, 0)
    rows_done(2 * 8 * layers, load_sem.at[3])

    for step in range(STEPS):
        last = step == STEPS - 1
        speed_old, speed_new = speeds[step], speeds[step + 1]
        stress_old, stress_new = stresses[step], stresses[step + 1]

        def stress_of(chunk):
            halo_chunk(step, chunk)
            stress_chunk(step, chunk, speed_new, stress_old, stress_new)

        def push_of(chunk):
            if not last:
                push_chunk(step + 1, chunk, stress_new, speed_new)
                start_chunk(step + 1, chunk)

        columns_arrive(step, 0)
        rows_arrive(step, 0)
        join_chunk(step, 0, speed_new)
        rows_arrive(step, 1)
        corners_arrive(step, 0)
        join_chunk(step, 1, speed_new)
        ocean_level(step)
        stress_of(0)
        columns_arrive(step, 1)

        def body(turn, carry):
            rows_arrive(step, turn)
            pl.when(turn == 3)(lambda: corners_arrive(step, 1))
            join_chunk(step, turn, speed_new)
            stress_of(turn - 1)
            push_of(turn - 2)

            @pl.when(turn == 2)
            def _():
                ocean_flux(step)
                if not last:
                    ocean_prepare(step + 1)

            return carry

        lax.fori_loop(2, chunks, body, 0)
        stress_of(chunks - 1)
        push_of(chunks - 2)
        push_of(chunks - 1)

    for item in range(3):
        ocean_out[item] = sea[STEPS, item]
    drain()


def hand_on(waves, sea, waves_out, sea_out, sem):
    copies = [
        pltpu.make_async_copy(waves, waves_out, sem.at[0]),
        pltpu.make_async_copy(sea, sea_out, sem.at[1]),
    ]
    for copy in copies:
        copy.start()
    for copy in copies:
        copy.wait()


def solution(mesh):
    counts = (mesh.shape["gx"], mesh.shape["gy"])

    def local(*arrays):
        fields, ocean = arrays[0], arrays[4]
        layers = fields.shape[1]
        chunks = layers // CHUNK
        f32, dma = jnp.float32, pltpu.SemaphoreType.DMA
        cube = (layers, *TILE)
        padded = (layers + 4, *TILE)
        waves, sea = pl.pallas_call(
            functools.partial(kernel, counts),
            out_shape=(pltpu.VMEM(fields.shape, f32), pltpu.VMEM(ocean.shape, f32)),
            in_specs=[pl.BlockSpec(memory_space=pl.ANY)] * 8,
            out_specs=(
                pl.BlockSpec(memory_space=pltpu.VMEM),
                pl.BlockSpec(memory_space=pltpu.VMEM),
            ),
            scratch_shapes=[
                pltpu.VMEM((9, *padded), f32),
                pltpu.VMEM((6, *padded), f32),
                pltpu.VMEM((3, *padded), f32),
                pltpu.VMEM((3, *padded), f32),
                pltpu.VMEM(cube, f32),
                pltpu.VMEM(cube, f32),
                pltpu.VMEM(cube, f32),
                pltpu.VMEM((STEPS + 1, 3, *TILE), f32),
                pltpu.VMEM(TILE, f32),
                pltpu.VMEM(TILE, jnp.int32),
                pltpu.VMEM(TILE, jnp.int32),
                pltpu.VMEM((STEPS, *TILE), f32),
                pltpu.VMEM((STEPS, 3, *cube), f32),
                pltpu.VMEM((STEPS, 3, *cube), f32),
                pltpu.VMEM((STEPS, chunks, 3, *TILE), f32),
                pltpu.VMEM((STEPS, 5, *TILE), f32),
                pltpu.VMEM((STEPS, *TILE), f32),
                pltpu.VMEM((STEPS, 3, *cube), f32),
                pltpu.VMEM((STEPS, 3, *cube), f32),
                pltpu.VMEM(cube, f32),
                pltpu.VMEM((STEPS, 2, chunks, 2, *TILE), f32),
                pltpu.VMEM((STEPS, 4, chunks, *TILE), f32),
                pltpu.VMEM((STEPS, 5, *TILE), f32),
                pltpu.VMEM((STEPS, 2, *TILE), f32),
                pltpu.VMEM((STEPS, 4, *TILE), f32),
                pltpu.VMEM((3, *cube), f32),
                pltpu.VMEM((STEPS, chunks, *TILE), f32),
                pltpu.VMEM((STEPS, 5, *TILE), f32),
                pltpu.VMEM((STEPS, 3, *TILE), f32),
                pltpu.VMEM((9 * layers * 8, 128), f32),
                dma((4,)),
                dma((2,)),
                dma((STEPS, 2, chunks)),
                dma((2,)),
                dma((STEPS, 2, chunks // 2)),
                dma((4,)),
                dma((STEPS, 4, chunks // 2)),
            ],
            compiler_params=pltpu.CompilerParams(
                collective_id=0, has_side_effects=True, vmem_limit_bytes=60 << 20
            ),
            name="waves",
        )(*arrays)
        return pl.pallas_call(
            hand_on,
            out_shape=(
                jax.ShapeDtypeStruct(fields.shape, f32),
                jax.ShapeDtypeStruct(ocean.shape, f32),
            ),
            in_specs=[pl.BlockSpec(memory_space=pltpu.VMEM)] * 2,
            out_specs=(pl.BlockSpec(memory_space=pl.ANY), pl.BlockSpec(memory_space=pl.ANY)),
            scratch_shapes=[dma((2,))],
            compiler_params=pltpu.CompilerParams(vmem_limit_bytes=12 << 20),
            name="hand_on",
        )(waves, sea)

    flat = P("gy", "gx")
    deep = P(None, "gy", "gx")
    in_specs = (P(None, None, "gy", "gx"), deep, deep, deep, deep, flat, flat, flat)
    out_specs = (P(None, None, "gy", "gx"), deep)
    return jax.shard_map(local, mesh=mesh, in_specs=in_specs, out_specs=out_specs, check_vma=False)
```

```python
import functools

import jax
import jax.numpy as jnp
from jax import lax
from jax.experimental import pallas as pl
from jax.experimental.pallas import tpu as pltpu
from jax.sharding import PartitionSpec as P

STEPS = 2
CHUNK = 4
PACK = 8
TILE = (8, 128)

near = 9.0 / 8.0
far = -1.0 / 24.0
courant = 0.3
ocean_rate = 0.3
uplift = 0.5
loading = 0.5
viscous = 0.1

XX, YY, ZZ, XY, XZ, YZ = range(6)
ALONG_X = ((XX, True), (XY, False), (XZ, False))
ALONG_Y = ((XY, False), (YY, True), (YZ, False))
FIELD = (0, 2, 1)
ALONG_Z = ((XZ, False), (YZ, False), (ZZ, True))


def turned(tile, shift, axis):
    return pltpu.roll(tile, shift % tile.shape[axis], axis)


def kernel(
    counts,
    fields_ref,
    lame_ref,
    shear_ref,
    buoy_ref,
    ocean_ref,
    depth_ref,
    index_ref,
    wet_ref,
    wave_out,
    ocean_out,
    given,
    stress_b,
    speed_b,
    speed_c,
    lame,
    shear,
    buoy,
    sea,
    depth,
    index,
    wet_i,
    press,
    pushed,
    wraps,
    packs,
    rows_o,
    packs_o,
    halo_wraps,
    halo_pushed,
    halo_buoy,
    halo_x,
    halo_d,
    halo_oy,
    halo_ox,
    halo_od,
    speed_rows,
    speed_cols,
    cols_o,
    seafloor,
    edges,
    sized,
    load_sem,
    send_y,
    recv_y,
    send_x,
    recv_x,
    send_d,
    recv_d,
):
    count_x, count_y = counts
    at_x, at_y = lax.axis_index("gx"), lax.axis_index("gy")
    layers = fields_ref.shape[1]
    chunks = layers // CHUNK
    pairs = layers // PACK

    next_x = (jnp.minimum(at_x + 1, count_x - 1), jnp.maximum(at_x - 1, 0))
    next_y = (jnp.minimum(at_y + 1, count_y - 1), jnp.maximum(at_y - 1, 0))
    inside_x = (at_x < count_x - 1, at_x > 0)
    inside_y = (at_y < count_y - 1, at_y > 0)
    to_y = tuple({"gy": y} for y in next_y)
    to_x = tuple({"gx": x} for x in next_x)
    to_d = tuple({"gx": next_x[d // 2], "gy": next_y[d % 2]} for d in range(4))
    inside_d = tuple(jnp.logical_and(inside_x[d // 2], inside_y[d % 2]) for d in range(4))

    def each(inside, act):
        for direction, there in enumerate(inside):
            pl.when(there)(functools.partial(act, direction))

    def when(condition, act):
        if isinstance(condition, bool):
            if condition:
                act()
        else:
            pl.when(condition)(act)

    from_x = inside_x[::-1]
    from_y = inside_y[::-1]
    from_d = inside_d[::-1]

    barrier = pltpu.get_barrier_semaphore()
    for inside, to in ((inside_y, to_y), (inside_d, to_d), (inside_x, to_x)):
        each(
            inside,
            lambda d, to=to: pl.semaphore_signal(barrier, inc=1, device_id=to[d]),
        )

    def rows_done(count, semaphore):
        part = sized.at[pl.ds(0, count)]
        pltpu.make_async_copy(part, part, semaphore).wait()

    inner_layers = pl.ds(2, layers)
    for source, target, place in (
        (fields_ref, given.at[:, inner_layers], 0),
        (buoy_ref, buoy, 1),
        (ocean_ref, sea.at[0], 2),
        (depth_ref, depth, 2),
        (index_ref, index, 2),
        (wet_ref, wet_i, 2),
        (lame_ref, lame, 3),
        (shear_ref, shear, 3),
    ):
        pltpu.make_async_copy(source, target, load_sem.at[place]).start()
    stress_a, speed_a = given.at[pl.ds(3, 6)], given.at[pl.ds(0, 3)]

    none = jnp.zeros(TILE, jnp.float32)
    row_at = lax.broadcasted_iota(jnp.int32, TILE, 0)
    lane_at = lax.broadcasted_iota(jnp.int32, TILE, 1)
    group_at = lane_at // 4
    slot_at = lane_at % 4
    low_slot = slot_at < 2
    upper = row_at < 4
    edge_rows = jnp.logical_or(row_at < 2, row_at >= 6)
    edge_lanes = jnp.logical_or(lane_at < 2, lane_at >= 126)
    wrap_back = jnp.logical_or(row_at < 2, row_at >= 7)
    wrap_ahead = jnp.logical_or(row_at < 1, row_at >= 6)
    wrap_rows = (wrap_back, wrap_ahead, wrap_back)

    for step in range(STEPS):
        for item in range(3):
            seafloor[step, item] = none
    margins = (0, 1, layers + 2, layers + 3)
    for z in margins:
        for field in (XZ, YZ, ZZ):
            stress_a[field, z] = none
            stress_b[field, z] = none
        for field in range(3):
            speed_b[field, z] = none
            speed_c[field, z] = none

    wrap_parts = ((pl.ds(0, 2), (pl.ds(0, 2), pl.ds(7, 1))), (pl.ds(2, 1), (pl.ds(0, 1), pl.ds(6, 2))))
    push_parts = ((pl.ds(0, 2), (pl.ds(7, 1), pl.ds(0, 2))), (pl.ds(2, 1), (pl.ds(6, 2), pl.ds(0, 1))))

    def rows_copies(step, direction, chunk):
        result = []
        span = pl.ds(chunk * CHUNK, CHUNK)

        def add(source, target):
            result.append(
                pltpu.make_async_remote_copy(
                    source,
                    target,
                    send_y.at[direction],
                    recv_y.at[step, direction, chunk],
                    device_id=to_y[direction],
                )
            )

        for source, target, parts in (
            (wraps, halo_wraps, wrap_parts),
            (pushed, halo_pushed, push_parts),
        ):
            for fields, rows in parts:
                box = (step, fields, span, rows[direction], slice(None))
                add(source.at[box], target.at[box])
        if step == 0:
            box = (span, pl.ds(6, 2) if direction == 0 else pl.ds(0, 2), slice(None))
            add(buoy_ref.at[box], halo_buoy.at[box])
        return result

    def rows_arrive(step, chunk):
        count = (11 if step == 0 else 9) * CHUNK + (5 if isinstance(chunk, int) and chunk == 3 else 0)
        each(from_y, lambda d: rows_done(count, recv_y.at[step, d, chunk]))

    def columns_arrive(step, half):
        count = 32 + (8 if half == 1 else 0)
        each(from_x, lambda d: rows_done(count, recv_x.at[step, d, half]))

    def corners_arrive(step, pair):
        count = 12 if pair == 1 else 4
        each(from_d, lambda d: rows_done(count, recv_d.at[step, d, pair]))

    def columns_copy(step, direction, half):
        return pltpu.make_async_remote_copy(
            packs.at[step, pl.ds(2 * half, 2), pl.ds(0, 2)],
            halo_x.at[step, direction, pl.ds(2 * half, 2)],
            send_x.at[direction],
            recv_x.at[step, direction, half],
            device_id=to_x[direction],
        )

    def corner_copy(step, corner, pair):
        rows = pl.ds(4, 4) if corner % 2 == 0 else pl.ds(0, 4)
        return pltpu.make_async_remote_copy(
            packs.at[step, pair, 2, rows, :],
            halo_d.at[step, corner, pair, rows, :],
            send_d.at[corner],
            recv_d.at[step, corner, pair],
            device_id=to_d[corner],
        )

    def ocean_rows(step, direction):
        row = pl.ds(7, 1) if direction == 0 else pl.ds(0, 1)
        return pltpu.make_async_remote_copy(
            rows_o.at[step, :, row, :],
            halo_oy.at[step, :, row, :],
            send_y.at[direction],
            recv_y.at[step, direction, 3],
            device_id=to_y[direction],
        )

    def ocean_columns(step, direction):
        return pltpu.make_async_remote_copy(
            packs_o.at[step],
            halo_ox.at[step, direction],
            send_x.at[direction],
            recv_x.at[step, direction, 1],
            device_id=to_x[direction],
        )

    def ocean_corner(step, corner):
        return pltpu.make_async_remote_copy(
            packs_o.at[step],
            halo_od.at[step, corner],
            send_d.at[corner],
            recv_d.at[step, corner, 1],
            device_id=to_d[corner],
        )

    def start_chunk(step, chunk):
        def start_rows(direction):
            for copy in rows_copies(step, direction, chunk):
                copy.start()
            when(chunk == 3, lambda: ocean_rows(step, direction).start())

        each(inside_y, start_rows)

    def start_pair(step, pair):
        def start_corner(corner):
            corner_copy(step, corner, pair).start()
            when(pair == 1, lambda: ocean_corner(step, corner).start())

        def start_columns(half):
            def start(direction):
                columns_copy(step, direction, half).start()
                if half == 1:
                    ocean_columns(step, direction).start()

            each(inside_x, start)

        each(inside_d, start_corner)
        when(pair == 1, lambda: start_columns(0))
        when(pair == 3, lambda: start_columns(1))

    def drain():
        rows_y = STEPS * (9 * layers + 5) + 2 * layers
        rows_x = STEPS * (2 * pairs + 1) * 8
        rows_d = STEPS * (4 * pairs + 8)
        each(inside_y, lambda d: rows_done(rows_y, send_y.at[d]))
        each(inside_d, lambda d: rows_done(rows_d, send_d.at[d]))
        each(inside_x, lambda d: rows_done(rows_x, send_x.at[d]))

    def clear_rows(direction):
        first = direction == 0
        push_rows = slice(6, 8) if first else slice(0, 2)
        wrap_rows = slice(0, 2) if first else slice(6, 8)
        zeros = jnp.zeros((2, 128), jnp.float32)

        def clear(z, carry):
            halo_buoy[z, push_rows, :] = zeros
            for step in range(STEPS):
                for field in range(3):
                    halo_pushed[step, field, z, push_rows, :] = zeros
                    halo_wraps[step, field, z, wrap_rows, :] = zeros
            return carry

        lax.fori_loop(0, layers, clear, 0)
        for step in range(STEPS):
            for item in range(5):
                halo_oy[step, item, push_rows, :] = zeros

    def clear_columns(direction):
        for step in range(STEPS):
            halo_ox[step, direction] = none
            for pair in range(pairs):
                for part in range(2):
                    halo_x[step, direction, pair, part] = none

    def clear_corner(corner):
        for step in range(STEPS):
            halo_od[step, corner] = none
            for pair in range(pairs):
                halo_d[step, corner, pair] = none

    each(tuple(jnp.logical_not(there) for there in from_y), clear_rows)
    each(tuple(jnp.logical_not(there) for there in from_x), clear_columns)
    each(tuple(jnp.logical_not(there) for there in from_d), clear_corner)

    def packed(held, tile, place):
        return jnp.where(group_at == place, turned(tile, 2 + 4 * place, 1), held)

    def unpacked(part, place):
        return turned(part, -(2 + 4 * place), 1)

    def shifted(tile, halo, axis, by):
        at, size = (row_at, 8) if axis == 0 else (lane_at, 128)
        from_halo = at >= size - by if by > 0 else at < -by
        return turned(jnp.where(from_halo, halo, tile), by, axis)

    def differ(tile, halo, axis, forward):
        before = shifted(tile, halo, axis, 1)
        after = shifted(tile, halo, axis, -1)
        if forward:
            after_two = shifted(tile, halo, axis, -2)
            return near * (after - tile) + far * (after_two - before)
        before_two = shifted(tile, halo, axis, 2)
        return near * (tile - before) + far * (after - before_two)

    def differ_z(ref, field, z, forward):
        at = [ref[field, z + 2 + k] for k in ((-1, 0, 1, 2) if forward else (-2, -1, 0, 1))]
        return near * (at[2] - at[1]) + far * (at[3] - at[0])

    def weight(mask, value):
        return jnp.where(mask, jnp.float32(value), jnp.float32(0.0))

    def wrapped(tile, axis, forward, low_one, low_two, high_one, high_two):
        before, after = turned(tile, 1, axis), turned(tile, -1, axis)
        if forward:
            return (
                weight(low_one, -far) * before
                + weight(high_one, near) * after
                + weight(high_two, far) * turned(tile, -2, axis)
            )
        return (
            weight(low_one, -near) * before
            + weight(low_two, -far) * turned(tile, 2, axis)
            + weight(high_one, far) * after
        )

    row_ends = (row_at < 1, row_at < 2, row_at >= 7, row_at >= 6)
    slot_ends = (slot_at == 2, slot_at >= 2, slot_at == 1, slot_at < 2)

    def circular_y(tile, forward):
        before, after = turned(tile, 1, 0), turned(tile, -1, 0)
        low_one, low_two, high_one, high_two = row_ends
        if forward:
            two = turned(tile, -2, 0)
            whole = near * (after - tile) + far * (two - before)
            wrap = (
                weight(low_one, -far) * before
                + weight(high_one, near) * after
                + weight(high_two, far) * two
            )
        else:
            two = turned(tile, 2, 0)
            whole = near * (tile - before) + far * (after - two)
            wrap = (
                weight(low_one, -near) * before
                + weight(low_two, -far) * two
                + weight(high_one, far) * after
            )
        return whole - wrap, wrap

    def local_x(tile, forward):
        before, after = turned(tile, 1, 1), turned(tile, -1, 1)
        if forward:
            two = turned(tile, -2, 1)
            return (
                weight(lane_at < 127, near) * after
                - near * tile
                + weight(lane_at < 126, far) * two
                - weight(lane_at >= 1, far) * before
            )
        two = turned(tile, 2, 1)
        return (
            near * tile
            - weight(lane_at >= 1, near) * before
            + weight(lane_at < 127, far) * after
            - weight(lane_at >= 2, far) * two
        )

    def push_chunk(step, pair, sub, stress, speed):
        if sub == 0:
            edge_push = none if step == 0 else packs[0, pair, 0]
            edge_x, edge_y = none, none
        else:
            edge_push, edge_x, edge_y = packs[step, pair, 0], edges[0], edges[1]
        for inner in range(CHUNK):
            place = sub * CHUNK + inner
            z = pair * PACK + place
            rate = courant * buoy[z]
            if step == 0:
                edge_push = packed(edge_push, rate, 3 * PACK + place)
            for axis in range(3):
                tile_x, tile_y = stress[ALONG_X[axis][0], z + 2], stress[ALONG_Y[axis][0], z + 2]
                kept, wrap = circular_y(tile_y, ALONG_Y[axis][1])
                total = (
                    local_x(tile_x, ALONG_X[axis][1])
                    + kept
                    + differ_z(stress, ALONG_Z[axis][0], z, ALONG_Z[axis][1])
                )
                push = speed[axis, z + 2] + rate * total
                pushed[step, FIELD[axis], z] = push
                wraps[step, FIELD[axis], z] = wrap
                edge_push = packed(edge_push, push, axis * PACK + place)
                edge_x = packed(edge_x, tile_x, axis * PACK + place)
                edge_y = packed(edge_y, tile_y, axis * PACK + place)
        packs[step, pair, 0] = edge_push
        if sub == 0:
            edges[0], edges[1] = edge_x, edge_y
            return
        first = lane_at < 4 * PACK
        second = jnp.logical_and(lane_at >= 4 * PACK, lane_at < 8 * PACK)
        wrap_x = jnp.where(
            first, wrapped(edge_x, 1, True, *slot_ends), wrapped(edge_x, 1, False, *slot_ends)
        )
        packs[step, pair, 1] = wrap_x
        wrap_y = jnp.where(
            second, wrapped(edge_y, 0, True, *row_ends), wrapped(edge_y, 0, False, *row_ends)
        )
        packs[step, pair, 2] = jnp.where(edge_rows, wrap_x, turned(wrap_y, 4, 0))

    def join_chunk(step, pair, sub, speed):
        floor = none
        side = jnp.where(low_slot, halo_x[step, 1, pair, 1], halo_x[step, 0, pair, 1])
        for inner in range(CHUNK):
            place = sub * CHUNK + inner
            z = pair * PACK + place
            rate = courant * buoy[z]
            for axis in range(3):
                added = jnp.where(wrap_rows[axis], halo_wraps[step, FIELD[axis], z], 0.0) + jnp.where(
                    edge_lanes, unpacked(side, axis * PACK + place), 0.0
                )
                new = pushed[step, FIELD[axis], z] + rate * added
                speed[axis, z + 2] = new
                if axis == 2:
                    floor = floor + jnp.where(index[...] == z, new, 0.0)
                if step == STEPS - 1:
                    wave_out[axis, z] = new
        seafloor[step, 0] = seafloor[step, 0] + floor

    def corners(step, pair):
        def of(dx):
            return jnp.where(
                upper, halo_d[step, 2 * dx + 1, pair], halo_d[step, 2 * dx, pair]
            )

        low, high = of(0), of(1)
        wrap_y = turned(jnp.where(low_slot, low, high), 4, 0)
        return jnp.where(low_slot, high, low), jnp.where(edge_rows, wrap_y, 0.0)

    def halo_chunk(step, pair, sub):
        wrap_x, wrap_y = corners(step, pair)
        if sub == 0:
            edge = jnp.where(low_slot, halo_x[step, 0, pair, 0], halo_x[step, 1, pair, 0])
            span = lane_at // (4 * PACK)
            rate_edge = jnp.where(
                span == 0,
                turned(edge, 4 * PACK, 1),
                jnp.where(span == 1, turned(edge, 8 * PACK, 1), turned(edge, 12 * PACK, 1)),
            )
            speed_cols[step, pair] = edge + rate_edge * (packs[step, pair, 1] + wrap_y)
        for inner in range(CHUNK):
            place = sub * CHUNK + inner
            z = pair * PACK + place
            rate = courant * halo_buoy[z]
            for axis in range(3):
                added = wraps[step, FIELD[axis], z] + jnp.where(
                    edge_lanes, unpacked(wrap_x, axis * PACK + place), 0.0
                )
                speed_rows[axis, z] = halo_pushed[step, FIELD[axis], z] + rate * added

    def stress_chunk(step, pair, sub, speed, stress_old, stress_new, pressed):
        side = speed_cols[step, pair]
        floor_rows, floor_cols = none, none
        for inner in range(CHUNK):
            place = sub * CHUNK + inner
            z = pair * PACK + place
            vx, vy, vz = speed[0, z + 2], speed[1, z + 2], speed[2, z + 2]
            hx = [unpacked(side, axis * PACK + place) for axis in range(3)]
            hy = [speed_rows[axis, z] for axis in range(3)]
            if pressed:
                floor_rows = floor_rows + jnp.where(halo_oy[step, 4] == z, hy[2], 0.0)
                floor_cols = floor_cols + jnp.where(cols_o[step, 4] == z, hx[2], 0.0)
            strain_x = differ(vx, hx[0], 1, False)
            strain_y = differ(vy, hy[1], 0, False)
            strain_z = differ_z(speed, 2, z, False)
            shear_xy = differ(vx, hy[0], 0, True) + differ(vy, hx[1], 1, True)
            shear_xz = differ_z(speed, 0, z, True) + differ(vz, hx[2], 1, True)
            shear_yz = differ_z(speed, 1, z, True) + differ(vz, hy[2], 0, True)
            rate = courant * shear[z]
            bulk = (courant * lame[z]) * (strain_x + strain_y + strain_z)
            twice = 2.0 * rate
            new = {
                XX: stress_old[XX, z + 2] + (bulk + twice * strain_x),
                YY: stress_old[YY, z + 2] + (bulk + twice * strain_y),
                ZZ: stress_old[ZZ, z + 2] + (bulk + twice * strain_z),
                XY: stress_old[XY, z + 2] + rate * shear_xy,
                XZ: stress_old[XZ, z + 2] + rate * shear_xz,
                YZ: stress_old[YZ, z + 2] + rate * shear_yz,
            }
            if pressed:
                new[ZZ] = new[ZZ] - jnp.where(index[...] == z, press[step], 0.0)
            for field, value in new.items():
                if step == STEPS - 1:
                    wave_out[3 + field, z] = value
                else:
                    stress_new[field, z + 2] = value
        if pressed:
            seafloor[step, 1] = seafloor[step, 1] + floor_rows
            seafloor[step, 2] = seafloor[step, 2] + floor_cols

    def centred(tile, halo, axis):
        return 0.5 * (shifted(tile, halo, axis, -1) - shifted(tile, halo, axis, 1))

    def around(tile, rows, cols):
        return (
            shifted(tile, cols, 1, -1)
            + shifted(tile, cols, 1, 1)
            + shifted(tile, rows, 0, -1)
            + shifted(tile, rows, 0, 1)
            - 4.0 * tile
        )

    def ocean_prepare(step):
        level, flux_x, flux_y = sea[step, 0], sea[step, 1], sea[step, 2]
        wet = wet_i[...].astype(jnp.float32)
        spread = centred(flux_x, none, 1) + centred(flux_y, none, 0)
        items = (
            flux_x,
            flux_y,
            level - ocean_rate * (wet * spread),
            wet,
            index[...].astype(jnp.float32),
        )
        pack = none
        for place, item in enumerate(items):
            rows_o[step, place] = item
            pack = packed(pack, item, place)
        packs_o[step] = pack

    def ocean_level(step):
        level, flux_x, flux_y = sea[step, 0], sea[step, 1], sea[step, 2]
        wet = wet_i[...].astype(jnp.float32)
        edge = jnp.where(low_slot, halo_ox[step, 0], halo_ox[step, 1])
        cols = [unpacked(edge, item) for item in range(5)]
        for item in range(5):
            cols_o[step, item] = cols[item]
        spread = centred(flux_x, cols[0], 1) + centred(flux_y, halo_oy[step, 1], 0)
        level = level + wet * (uplift * seafloor[step, 0] - ocean_rate * spread)
        sea[step + 1, 0] = level
        press[step] = loading * (wet * level)

    def press_late(step, stress_new):
        floor_rows, floor_cols = none, none
        for z in range(2 * CHUNK):
            edge = unpacked(speed_cols[step, 0], 2 * PACK + z)
            floor_rows = floor_rows + jnp.where(halo_oy[step, 4] == z, speed_rows[2, z], 0.0)
            floor_cols = floor_cols + jnp.where(cols_o[step, 4] == z, edge, 0.0)
            less = jnp.where(index[...] == z, press[step], 0.0)
            if step == STEPS - 1:
                wave_out[3 + ZZ, z] = wave_out[3 + ZZ, z] - less
            else:
                stress_new[ZZ, z + 2] = stress_new[ZZ, z + 2] - less
        seafloor[step, 1] = floor_rows
        seafloor[step, 2] = floor_cols

    def ocean_flux(step):
        level, flux_x, flux_y = sea[step + 1, 0], sea[step, 1], sea[step, 2]
        wet = wet_i[...].astype(jnp.float32)

        def of(dx):
            return jnp.where(upper, halo_od[step, 2 * dx + 1], halo_od[step, 2 * dx])

        corner = jnp.where(low_slot, of(0), of(1))

        spread = centred(none, flux_y, 0) + centred(none, unpacked(corner, 0), 1)
        level_rows = halo_oy[step, 2] + halo_oy[step, 3] * (
            uplift * seafloor[step, 1] - ocean_rate * spread
        )
        spread = centred(none, flux_x, 1) + centred(none, unpacked(corner, 1), 0)
        level_cols = cols_o[step, 2] + cols_o[step, 3] * (
            uplift * seafloor[step, 2] - ocean_rate * spread
        )
        slope_x = centred(level, level_cols, 1)
        slope_y = centred(level, level_rows, 0)
        around_x = around(flux_x, halo_oy[step, 0], cols_o[step, 0])
        around_y = around(flux_y, halo_oy[step, 1], cols_o[step, 1])
        pull = ocean_rate * depth[...]
        sea[step + 1, 1] = wet * (flux_x - pull * slope_x + viscous * around_x)
        sea[step + 1, 2] = wet * (flux_y - pull * slope_y + viscous * around_y)

    for count, place in ((9 * 8 * layers, 0), (8 * layers, 1), (6 * 8, 2)):
        rows_done(count, load_sem.at[place])
    speeds = (speed_a, speed_b, speed_c)
    stresses = (stress_a, stress_b, stress_b)

    def first_push(pair, carry):
        for sub in range(2):
            push_chunk(0, pair, sub, stress_a, speed_a)
        return carry

    lax.fori_loop(0, 2, first_push, 0)
    ocean_prepare(0)

    peers = sum(there.astype(jnp.int32) for there in (*inside_x, *inside_y, *inside_d))
    pl.semaphore_wait(barrier, peers)

    def first_send(pair, carry):
        for sub in range(2):
            start_chunk(0, 2 * pair + sub)
        start_pair(0, pair)
        return carry

    def paced(pair, carry):
        first_send(pair - 2, carry)
        return first_push(pair, carry)

    lax.fori_loop(2, pairs, paced, 0)
    lax.fori_loop(pairs - 2, pairs, first_send, 0)
    rows_done(2 * 8 * layers, load_sem.at[3])

    for step in range(STEPS):
        last = step == STEPS - 1
        speed_old, speed_new = speeds[step], speeds[step + 1]
        stress_old, stress_new = stresses[step], stresses[step + 1]

        def join_of(pair, sub):
            rows_arrive(step, 2 * pair + sub)
            join_chunk(step, pair, sub, speed_new)

        def stress_of(pair, sub, pressed=True):
            halo_chunk(step, pair, sub)
            stress_chunk(step, pair, sub, speed_new, stress_old, stress_new, pressed)

        def push_of(pair, sub):
            if not last:
                push_chunk(step + 1, pair, sub, stress_new, speed_new)
                start_chunk(step + 1, 2 * pair + sub)
                if sub == 1:
                    start_pair(step + 1, pair)

        columns_arrive(step, 0)
        join_of(0, 0)
        join_of(0, 1)
        corners_arrive(step, 0)
        stress_of(0, 0, False)
        join_of(1, 0)
        stress_of(0, 1, False)
        columns_arrive(step, 1)
        corners_arrive(step, 1)
        join_of(1, 1)
        ocean_level(step)
        press_late(step, stress_new)
        stress_of(1, 0)
        push_of(0, 0)
        push_of(0, 1)
        for pair in range(2, pairs):
            join_of(pair, 0)
            stress_of(pair - 1, 1)
            push_of(pair - 1, 0)
            if pair == 2:
                ocean_flux(step)
                if not last:
                    ocean_prepare(step + 1)
            corners_arrive(step, pair)
            join_of(pair, 1)
            stress_of(pair, 0)
            push_of(pair - 1, 1)
        stress_of(pairs - 1, 1)
        push_of(pairs - 1, 0)
        push_of(pairs - 1, 1)

    for item in range(3):
        ocean_out[item] = sea[STEPS, item]
    drain()


def hand_on(waves, sea, waves_out, sea_out, sem):
    copies = [
        pltpu.make_async_copy(waves, waves_out, sem.at[0]),
        pltpu.make_async_copy(sea, sea_out, sem.at[1]),
    ]
    for copy in copies:
        copy.start()
    for copy in copies:
        copy.wait()


def solution(mesh):
    counts = (mesh.shape["gx"], mesh.shape["gy"])

    def local(*arrays):
        fields, ocean = arrays[0], arrays[4]
        layers = fields.shape[1]
        chunks, pairs = layers // CHUNK, layers // PACK
        f32, dma = jnp.float32, pltpu.SemaphoreType.DMA
        cube = (layers, *TILE)
        padded = (layers + 4, *TILE)
        waves, sea = pl.pallas_call(
            functools.partial(kernel, counts),
            out_shape=(pltpu.VMEM(fields.shape, f32), pltpu.VMEM(ocean.shape, f32)),
            in_specs=[pl.BlockSpec(memory_space=pl.ANY)] * 8,
            out_specs=(
                pl.BlockSpec(memory_space=pltpu.VMEM),
                pl.BlockSpec(memory_space=pltpu.VMEM),
            ),
            scratch_shapes=[
                pltpu.VMEM((9, *padded), f32),
                pltpu.VMEM((6, *padded), f32),
                pltpu.VMEM((3, *padded), f32),
                pltpu.VMEM((3, *padded), f32),
                pltpu.VMEM(cube, f32),
                pltpu.VMEM(cube, f32),
                pltpu.VMEM(cube, f32),
                pltpu.VMEM((STEPS + 1, 3, *TILE), f32),
                pltpu.VMEM(TILE, f32),
                pltpu.VMEM(TILE, jnp.int32),
                pltpu.VMEM(TILE, jnp.int32),
                pltpu.VMEM((STEPS, *TILE), f32),
                pltpu.VMEM((STEPS, 3, *cube), f32),
                pltpu.VMEM((STEPS, 3, *cube), f32),
                pltpu.VMEM((STEPS, pairs, 3, *TILE), f32),
                pltpu.VMEM((STEPS, 5, *TILE), f32),
                pltpu.VMEM((STEPS, *TILE), f32),
                pltpu.VMEM((STEPS, 3, *cube), f32),
                pltpu.VMEM((STEPS, 3, *cube), f32),
                pltpu.VMEM(cube, f32),
                pltpu.VMEM((STEPS, 2, pairs, 2, *TILE), f32),
                pltpu.VMEM((STEPS, 4, pairs, *TILE), f32),
                pltpu.VMEM((STEPS, 5, *TILE), f32),
                pltpu.VMEM((STEPS, 2, *TILE), f32),
                pltpu.VMEM((STEPS, 4, *TILE), f32),
                pltpu.VMEM((3, *cube), f32),
                pltpu.VMEM((STEPS, pairs, *TILE), f32),
                pltpu.VMEM((STEPS, 5, *TILE), f32),
                pltpu.VMEM((STEPS, 3, *TILE), f32),
                pltpu.VMEM((2, *TILE), f32),
                pltpu.VMEM((9 * layers * 8, 128), f32),
                dma((4,)),
                dma((2,)),
                dma((STEPS, 2, chunks)),
                dma((2,)),
                dma((STEPS, 2, 2)),
                dma((4,)),
                dma((STEPS, 4, pairs)),
            ],
            compiler_params=pltpu.CompilerParams(
                collective_id=0, has_side_effects=True, vmem_limit_bytes=60 << 20
            ),
            name="waves",
        )(*arrays)
        return pl.pallas_call(
            hand_on,
            out_shape=(
                jax.ShapeDtypeStruct(fields.shape, f32),
                jax.ShapeDtypeStruct(ocean.shape, f32),
            ),
            in_specs=[pl.BlockSpec(memory_space=pltpu.VMEM)] * 2,
            out_specs=(pl.BlockSpec(memory_space=pl.ANY), pl.BlockSpec(memory_space=pl.ANY)),
            scratch_shapes=[dma((2,))],
            compiler_params=pltpu.CompilerParams(vmem_limit_bytes=12 << 20),
            name="hand_on",
        )(waves, sea)

    flat = P("gy", "gx")
    deep = P(None, "gy", "gx")
    in_specs = (P(None, None, "gy", "gx"), deep, deep, deep, deep, flat, flat, flat)
    out_specs = (P(None, None, "gy", "gx"), deep)
    return jax.shard_map(local, mesh=mesh, in_specs=in_specs, out_specs=out_specs, check_vma=False)
```

```python
import functools

import jax
import jax.numpy as jnp
from jax import lax
from jax.experimental import pallas as pl
from jax.experimental.pallas import tpu as pltpu
from jax.sharding import PartitionSpec as P

STEPS = 2
CHUNK = 4
PACK = 8
TILE = (8, 128)

near = -27.0
courant = 0.3 * (-1.0 / 24.0)
ocean_rate = 0.3
uplift = 0.5
loading = 0.5
viscous = 0.1

XX, YY, ZZ, XY, XZ, YZ = range(6)
ALONG_X = ((XX, True), (XY, False), (XZ, False))
ALONG_Y = ((XY, False), (YY, True), (YZ, False))
FIELD = (0, 2, 1)
ALONG_Z = ((XZ, False), (YZ, False), (ZZ, True))


def turned(tile, shift, axis):
    return pltpu.roll(tile, shift % tile.shape[axis], axis)


def kernel(
    counts,
    fields_ref,
    lame_ref,
    shear_ref,
    buoy_ref,
    ocean_ref,
    depth_ref,
    index_ref,
    wet_ref,
    wave_out,
    ocean_out,
    given,
    stress_b,
    speed_b,
    speed_c,
    lame,
    shear,
    buoy,
    sea,
    depth,
    index,
    wet_i,
    press,
    pushed,
    wraps,
    packs,
    rows_o,
    packs_o,
    halo_wraps,
    halo_pushed,
    halo_buoy,
    halo_x,
    halo_d,
    halo_oy,
    halo_ox,
    halo_od,
    speed_rows,
    speed_cols,
    cols_o,
    seafloor,
    edges,
    sized,
    load_sem,
    send_y,
    recv_y,
    send_x,
    recv_x,
    send_d,
    recv_d,
):
    count_x, count_y = counts
    at_x, at_y = lax.axis_index("gx"), lax.axis_index("gy")
    layers = fields_ref.shape[1]
    chunks = layers // CHUNK
    pairs = layers // PACK

    next_x = (jnp.minimum(at_x + 1, count_x - 1), jnp.maximum(at_x - 1, 0))
    next_y = (jnp.minimum(at_y + 1, count_y - 1), jnp.maximum(at_y - 1, 0))
    inside_x = (at_x < count_x - 1, at_x > 0)
    inside_y = (at_y < count_y - 1, at_y > 0)
    to_y = tuple({"gy": y} for y in next_y)
    to_x = tuple({"gx": x} for x in next_x)
    to_d = tuple({"gx": next_x[d // 2], "gy": next_y[d % 2]} for d in range(4))
    inside_d = tuple(jnp.logical_and(inside_x[d // 2], inside_y[d % 2]) for d in range(4))

    def each(inside, act):
        for direction, there in enumerate(inside):
            pl.when(there)(functools.partial(act, direction))

    def when(condition, act):
        if isinstance(condition, bool):
            if condition:
                act()
        else:
            pl.when(condition)(act)

    from_x = inside_x[::-1]
    from_y = inside_y[::-1]
    from_d = inside_d[::-1]

    barrier = pltpu.get_barrier_semaphore()
    for inside, to in ((inside_y, to_y), (inside_d, to_d), (inside_x, to_x)):
        each(
            inside,
            lambda d, to=to: pl.semaphore_signal(barrier, inc=1, device_id=to[d]),
        )

    def rows_done(count, semaphore):
        part = sized.at[pl.ds(0, count)]
        pltpu.make_async_copy(part, part, semaphore).wait()

    inner_layers = pl.ds(2, layers)
    for source, target, place in (
        (fields_ref, given.at[:, inner_layers], 0),
        (buoy_ref, buoy, 1),
        (ocean_ref, sea.at[0], 2),
        (depth_ref, depth, 2),
        (index_ref, index, 2),
        (wet_ref, wet_i, 2),
        (lame_ref, lame, 3),
        (shear_ref, shear, 3),
    ):
        pltpu.make_async_copy(source, target, load_sem.at[place]).start()
    stress_a, speed_a = given.at[pl.ds(3, 6)], given.at[pl.ds(0, 3)]

    none = jnp.zeros(TILE, jnp.float32)
    row_at = lax.broadcasted_iota(jnp.int32, TILE, 0)
    lane_at = lax.broadcasted_iota(jnp.int32, TILE, 1)
    group_at = lane_at // 4
    slot_at = lane_at % 4
    low_slot = slot_at < 2
    upper = row_at < 4
    edge_rows = jnp.logical_or(row_at < 2, row_at >= 6)
    edge_lanes = jnp.logical_or(lane_at < 2, lane_at >= 126)
    wrap_back = jnp.logical_or(row_at < 2, row_at >= 7)
    wrap_ahead = jnp.logical_or(row_at < 1, row_at >= 6)
    wrap_rows = (wrap_back, wrap_ahead, wrap_back)

    for step in range(STEPS):
        for item in range(3):
            seafloor[step, item] = none
    margins = (0, 1, layers + 2, layers + 3)
    for z in margins:
        for field in (XZ, YZ, ZZ):
            stress_a[field, z] = none
            stress_b[field, z] = none
        for field in range(3):
            speed_b[field, z] = none
            speed_c[field, z] = none

    wrap_parts = ((pl.ds(0, 2), (pl.ds(0, 2), pl.ds(7, 1))), (pl.ds(2, 1), (pl.ds(0, 1), pl.ds(6, 2))))
    push_parts = ((pl.ds(0, 2), (pl.ds(7, 1), pl.ds(0, 2))), (pl.ds(2, 1), (pl.ds(6, 2), pl.ds(0, 1))))

    def rows_copies(step, direction, chunk):
        result = []
        span = pl.ds(chunk * CHUNK, CHUNK)

        def add(source, target):
            result.append(
                pltpu.make_async_remote_copy(
                    source,
                    target,
                    send_y.at[direction],
                    recv_y.at[step, direction, chunk],
                    device_id=to_y[direction],
                )
            )

        for source, target, parts in (
            (wraps, halo_wraps, wrap_parts),
            (pushed, halo_pushed, push_parts),
        ):
            for fields, rows in parts:
                box = (step, fields, span, rows[direction], slice(None))
                add(source.at[box], target.at[box])
        if step == 0:
            box = (span, pl.ds(6, 2) if direction == 0 else pl.ds(0, 2), slice(None))
            add(buoy_ref.at[box], halo_buoy.at[box])
        return result

    def rows_arrive(step, chunk):
        count = (11 if step == 0 else 9) * CHUNK + (5 if isinstance(chunk, int) and chunk == 3 else 0)
        each(from_y, lambda d: rows_done(count, recv_y.at[step, d, chunk]))

    def columns_arrive(step, half):
        count = 32 + (8 if half == 1 else 0)
        each(from_x, lambda d: rows_done(count, recv_x.at[step, d, half]))

    def corners_arrive(step, pair):
        count = 12 if pair == 1 else 4
        each(from_d, lambda d: rows_done(count, recv_d.at[step, d, pair]))

    def columns_copy(step, direction, half):
        return pltpu.make_async_remote_copy(
            packs.at[step, pl.ds(2 * half, 2), pl.ds(0, 2)],
            halo_x.at[step, direction, pl.ds(2 * half, 2)],
            send_x.at[direction],
            recv_x.at[step, direction, half],
            device_id=to_x[direction],
        )

    def corner_copy(step, corner, pair):
        rows = pl.ds(4, 4) if corner % 2 == 0 else pl.ds(0, 4)
        return pltpu.make_async_remote_copy(
            packs.at[step, pair, 2, rows, :],
            halo_d.at[step, corner, pair, rows, :],
            send_d.at[corner],
            recv_d.at[step, corner, pair],
            device_id=to_d[corner],
        )

    def ocean_rows(step, direction):
        row = pl.ds(7, 1) if direction == 0 else pl.ds(0, 1)
        return pltpu.make_async_remote_copy(
            rows_o.at[step, :, row, :],
            halo_oy.at[step, :, row, :],
            send_y.at[direction],
            recv_y.at[step, direction, 3],
            device_id=to_y[direction],
        )

    def ocean_columns(step, direction):
        return pltpu.make_async_remote_copy(
            packs_o.at[step],
            halo_ox.at[step, direction],
            send_x.at[direction],
            recv_x.at[step, direction, 1],
            device_id=to_x[direction],
        )

    def ocean_corner(step, corner):
        return pltpu.make_async_remote_copy(
            packs_o.at[step],
            halo_od.at[step, corner],
            send_d.at[corner],
            recv_d.at[step, corner, 1],
            device_id=to_d[corner],
        )

    def start_chunk(step, chunk):
        def start_rows(direction):
            for copy in rows_copies(step, direction, chunk):
                copy.start()
            when(chunk == 3, lambda: ocean_rows(step, direction).start())

        each(inside_y, start_rows)

    def start_pair(step, pair):
        def start_corner(corner):
            corner_copy(step, corner, pair).start()
            when(pair == 1, lambda: ocean_corner(step, corner).start())

        def start_columns(half):
            def start(direction):
                columns_copy(step, direction, half).start()
                if half == 1:
                    ocean_columns(step, direction).start()

            each(inside_x, start)

        each(inside_d, start_corner)
        when(pair == 1, lambda: start_columns(0))
        when(pair == 3, lambda: start_columns(1))

    def drain():
        rows_y = STEPS * (9 * layers + 5) + 2 * layers
        rows_x = STEPS * (2 * pairs + 1) * 8
        rows_d = STEPS * (4 * pairs + 8)
        each(inside_y, lambda d: rows_done(rows_y, send_y.at[d]))
        each(inside_d, lambda d: rows_done(rows_d, send_d.at[d]))
        each(inside_x, lambda d: rows_done(rows_x, send_x.at[d]))

    def clear_rows(direction):
        first = direction == 0
        push_rows = slice(6, 8) if first else slice(0, 2)
        wrap_rows = slice(0, 2) if first else slice(6, 8)
        zeros = jnp.zeros((2, 128), jnp.float32)

        def clear(z, carry):
            halo_buoy[z, push_rows, :] = zeros
            for step in range(STEPS):
                for field in range(3):
                    halo_pushed[step, field, z, push_rows, :] = zeros
                    halo_wraps[step, field, z, wrap_rows, :] = zeros
            return carry

        lax.fori_loop(0, layers, clear, 0)
        for step in range(STEPS):
            for item in range(5):
                halo_oy[step, item, push_rows, :] = zeros

    def clear_columns(direction):
        for step in range(STEPS):
            halo_ox[step, direction] = none
            for pair in range(pairs):
                for part in range(2):
                    halo_x[step, direction, pair, part] = none

    def clear_corner(corner):
        for step in range(STEPS):
            halo_od[step, corner] = none
            for pair in range(pairs):
                halo_d[step, corner, pair] = none

    each(tuple(jnp.logical_not(there) for there in from_y), clear_rows)
    each(tuple(jnp.logical_not(there) for there in from_x), clear_columns)
    each(tuple(jnp.logical_not(there) for there in from_d), clear_corner)

    def packed(held, tile, place):
        return jnp.where(group_at == place, turned(tile, 2 + 4 * place, 1), held)

    def unpacked(part, place):
        return turned(part, -(2 + 4 * place), 1)

    def shifted(tile, halo, axis, by):
        at, size = (row_at, 8) if axis == 0 else (lane_at, 128)
        from_halo = at >= size - by if by > 0 else at < -by
        return turned(jnp.where(from_halo, halo, tile), by, axis)

    def differ(tile, halo, axis, forward):
        before = shifted(tile, halo, axis, 1)
        after = shifted(tile, halo, axis, -1)
        if forward:
            after_two = shifted(tile, halo, axis, -2)
            return near * (after - tile) + (after_two - before)
        before_two = shifted(tile, halo, axis, 2)
        return near * (tile - before) + (after - before_two)

    def differ_z(ref, field, z, forward):
        at = [ref[field, z + 2 + k] for k in ((-1, 0, 1, 2) if forward else (-2, -1, 0, 1))]
        return near * (at[2] - at[1]) + (at[3] - at[0])

    def weight(mask, value):
        return jnp.where(mask, jnp.float32(value), jnp.float32(0.0))

    def wrapped(tile, axis, forward, low_one, low_two, high_one, high_two):
        before, after = turned(tile, 1, axis), turned(tile, -1, axis)
        if forward:
            return (
                weight(low_one, -1.0) * before
                + weight(high_one, near) * after
                + weight(high_two, 1.0) * turned(tile, -2, axis)
            )
        return (
            weight(low_one, -near) * before
            + weight(low_two, -1.0) * turned(tile, 2, axis)
            + weight(high_one, 1.0) * after
        )

    row_ends = (row_at < 1, row_at < 2, row_at >= 7, row_at >= 6)
    slot_ends = (slot_at == 2, slot_at >= 2, slot_at == 1, slot_at < 2)

    def circular_y(tile, forward):
        before, after = turned(tile, 1, 0), turned(tile, -1, 0)
        low_one, low_two, high_one, high_two = row_ends
        if forward:
            two = turned(tile, -2, 0)
            whole = near * (after - tile) + (two - before)
            wrap = (
                weight(low_one, -1.0) * before
                + weight(high_one, near) * after
                + weight(high_two, 1.0) * two
            )
        else:
            two = turned(tile, 2, 0)
            whole = near * (tile - before) + (after - two)
            wrap = (
                weight(low_one, -near) * before
                + weight(low_two, -1.0) * two
                + weight(high_one, 1.0) * after
            )
        return whole - wrap, wrap

    def local_x(tile, forward):
        before, after = turned(tile, 1, 1), turned(tile, -1, 1)
        if forward:
            two = turned(tile, -2, 1)
            return (
                weight(lane_at < 127, near) * after
                - near * tile
                + jnp.where(lane_at < 126, two, 0.0)
                - jnp.where(lane_at >= 1, before, 0.0)
            )
        two = turned(tile, 2, 1)
        return (
            near * tile
            - weight(lane_at >= 1, near) * before
            + jnp.where(lane_at < 127, after, 0.0)
            - jnp.where(lane_at >= 2, two, 0.0)
        )

    def push_chunk(step, pair, sub, stress, speed):
        if sub == 0:
            edge_push = none if step == 0 else packs[0, pair, 0]
            edge_x, edge_y = none, none
        else:
            edge_push, edge_x, edge_y = packs[step, pair, 0], edges[0], edges[1]
        for inner in range(CHUNK):
            place = sub * CHUNK + inner
            z = pair * PACK + place
            rate = courant * buoy[z]
            if step == 0:
                edge_push = packed(edge_push, rate, 3 * PACK + place)
            for axis in range(3):
                tile_x, tile_y = stress[ALONG_X[axis][0], z + 2], stress[ALONG_Y[axis][0], z + 2]
                kept, wrap = circular_y(tile_y, ALONG_Y[axis][1])
                total = (
                    local_x(tile_x, ALONG_X[axis][1])
                    + kept
                    + differ_z(stress, ALONG_Z[axis][0], z, ALONG_Z[axis][1])
                )
                push = speed[axis, z + 2] + rate * total
                pushed[step, FIELD[axis], z] = push
                wraps[step, FIELD[axis], z] = wrap
                edge_push = packed(edge_push, push, axis * PACK + place)
                edge_x = packed(edge_x, tile_x, axis * PACK + place)
                edge_y = packed(edge_y, tile_y, axis * PACK + place)
        packs[step, pair, 0] = edge_push
        if sub == 0:
            edges[0], edges[1] = edge_x, edge_y
            return
        first = lane_at < 4 * PACK
        second = jnp.logical_and(lane_at >= 4 * PACK, lane_at < 8 * PACK)
        wrap_x = jnp.where(
            first, wrapped(edge_x, 1, True, *slot_ends), wrapped(edge_x, 1, False, *slot_ends)
        )
        packs[step, pair, 1] = wrap_x
        wrap_y = jnp.where(
            second, wrapped(edge_y, 0, True, *row_ends), wrapped(edge_y, 0, False, *row_ends)
        )
        packs[step, pair, 2] = jnp.where(edge_rows, wrap_x, turned(wrap_y, 4, 0))

    def join_chunk(step, pair, sub, speed):
        floor = none
        side = jnp.where(low_slot, halo_x[step, 1, pair, 1], halo_x[step, 0, pair, 1])
        for inner in range(CHUNK):
            place = sub * CHUNK + inner
            z = pair * PACK + place
            rate = courant * buoy[z]
            for axis in range(3):
                added = jnp.where(wrap_rows[axis], halo_wraps[step, FIELD[axis], z], 0.0) + jnp.where(
                    edge_lanes, unpacked(side, axis * PACK + place), 0.0
                )
                new = pushed[step, FIELD[axis], z] + rate * added
                speed[axis, z + 2] = new
                if axis == 2:
                    floor = floor + jnp.where(index[...] == z, new, 0.0)
                if step == STEPS - 1:
                    wave_out[axis, z] = new
        seafloor[step, 0] = seafloor[step, 0] + floor

    def corners(step, pair):
        def of(dx):
            return jnp.where(
                upper, halo_d[step, 2 * dx + 1, pair], halo_d[step, 2 * dx, pair]
            )

        low, high = of(0), of(1)
        wrap_y = turned(jnp.where(low_slot, low, high), 4, 0)
        return jnp.where(low_slot, high, low), jnp.where(edge_rows, wrap_y, 0.0)

    def halo_chunk(step, pair, sub):
        wrap_x, wrap_y = corners(step, pair)
        if sub == 0:
            edge = jnp.where(low_slot, halo_x[step, 0, pair, 0], halo_x[step, 1, pair, 0])
            span = lane_at // (4 * PACK)
            rate_edge = jnp.where(
                span == 0,
                turned(edge, 4 * PACK, 1),
                jnp.where(span == 1, turned(edge, 8 * PACK, 1), turned(edge, 12 * PACK, 1)),
            )
            speed_cols[step, pair] = edge + rate_edge * (packs[step, pair, 1] + wrap_y)
        for inner in range(CHUNK):
            place = sub * CHUNK + inner
            z = pair * PACK + place
            rate = courant * halo_buoy[z]
            for axis in range(3):
                added = wraps[step, FIELD[axis], z] + jnp.where(
                    edge_lanes, unpacked(wrap_x, axis * PACK + place), 0.0
                )
                speed_rows[axis, z] = halo_pushed[step, FIELD[axis], z] + rate * added

    def stress_chunk(step, pair, sub, speed, stress_old, stress_new, pressed):
        side = speed_cols[step, pair]
        floor_rows, floor_cols = none, none
        for inner in range(CHUNK):
            place = sub * CHUNK + inner
            z = pair * PACK + place
            vx, vy, vz = speed[0, z + 2], speed[1, z + 2], speed[2, z + 2]
            hx = [unpacked(side, axis * PACK + place) for axis in range(3)]
            hy = [speed_rows[axis, z] for axis in range(3)]
            if pressed:
                floor_rows = floor_rows + jnp.where(halo_oy[step, 4] == z, hy[2], 0.0)
                floor_cols = floor_cols + jnp.where(cols_o[step, 4] == z, hx[2], 0.0)
            strain_x = differ(vx, hx[0], 1, False)
            strain_y = differ(vy, hy[1], 0, False)
            strain_z = differ_z(speed, 2, z, False)
            shear_xy = differ(vx, hy[0], 0, True) + differ(vy, hx[1], 1, True)
            shear_xz = differ_z(speed, 0, z, True) + differ(vz, hx[2], 1, True)
            shear_yz = differ_z(speed, 1, z, True) + differ(vz, hy[2], 0, True)
            rate = courant * shear[z]
            bulk = (courant * lame[z]) * (strain_x + strain_y + strain_z)
            twice = 2.0 * rate
            new = {
                XX: stress_old[XX, z + 2] + (bulk + twice * strain_x),
                YY: stress_old[YY, z + 2] + (bulk + twice * strain_y),
                ZZ: stress_old[ZZ, z + 2] + (bulk + twice * strain_z),
                XY: stress_old[XY, z + 2] + rate * shear_xy,
                XZ: stress_old[XZ, z + 2] + rate * shear_xz,
                YZ: stress_old[YZ, z + 2] + rate * shear_yz,
            }
            if pressed:
                new[ZZ] = new[ZZ] - jnp.where(index[...] == z, press[step], 0.0)
            for field, value in new.items():
                if step == STEPS - 1:
                    wave_out[3 + field, z] = value
                else:
                    stress_new[field, z + 2] = value
        if pressed:
            seafloor[step, 1] = seafloor[step, 1] + floor_rows
            seafloor[step, 2] = seafloor[step, 2] + floor_cols

    def centred(tile, halo, axis):
        return 0.5 * (shifted(tile, halo, axis, -1) - shifted(tile, halo, axis, 1))

    def around(tile, rows, cols):
        return (
            shifted(tile, cols, 1, -1)
            + shifted(tile, cols, 1, 1)
            + shifted(tile, rows, 0, -1)
            + shifted(tile, rows, 0, 1)
            - 4.0 * tile
        )

    def ocean_prepare(step):
        level, flux_x, flux_y = sea[step, 0], sea[step, 1], sea[step, 2]
        wet = wet_i[...].astype(jnp.float32)
        spread = centred(flux_x, none, 1) + centred(flux_y, none, 0)
        items = (
            flux_x,
            flux_y,
            level - ocean_rate * (wet * spread),
            wet,
            index[...].astype(jnp.float32),
        )
        pack = none
        for place, item in enumerate(items):
            rows_o[step, place] = item
            pack = packed(pack, item, place)
        packs_o[step] = pack

    def ocean_level(step):
        level, flux_x, flux_y = sea[step, 0], sea[step, 1], sea[step, 2]
        wet = wet_i[...].astype(jnp.float32)
        edge = jnp.where(low_slot, halo_ox[step, 0], halo_ox[step, 1])
        cols = [unpacked(edge, item) for item in range(5)]
        for item in range(5):
            cols_o[step, item] = cols[item]
        spread = centred(flux_x, cols[0], 1) + centred(flux_y, halo_oy[step, 1], 0)
        level = level + wet * (uplift * seafloor[step, 0] - ocean_rate * spread)
        sea[step + 1, 0] = level
        press[step] = loading * (wet * level)

    def press_late(step, stress_new):
        floor_rows, floor_cols = none, none
        for z in range(2 * CHUNK):
            edge = unpacked(speed_cols[step, 0], 2 * PACK + z)
            floor_rows = floor_rows + jnp.where(halo_oy[step, 4] == z, speed_rows[2, z], 0.0)
            floor_cols = floor_cols + jnp.where(cols_o[step, 4] == z, edge, 0.0)
            less = jnp.where(index[...] == z, press[step], 0.0)
            if step == STEPS - 1:
                wave_out[3 + ZZ, z] = wave_out[3 + ZZ, z] - less
            else:
                stress_new[ZZ, z + 2] = stress_new[ZZ, z + 2] - less
        seafloor[step, 1] = floor_rows
        seafloor[step, 2] = floor_cols

    def ocean_flux(step):
        level, flux_x, flux_y = sea[step + 1, 0], sea[step, 1], sea[step, 2]
        wet = wet_i[...].astype(jnp.float32)

        def of(dx):
            return jnp.where(upper, halo_od[step, 2 * dx + 1], halo_od[step, 2 * dx])

        corner = jnp.where(low_slot, of(0), of(1))

        spread = centred(none, flux_y, 0) + centred(none, unpacked(corner, 0), 1)
        level_rows = halo_oy[step, 2] + halo_oy[step, 3] * (
            uplift * seafloor[step, 1] - ocean_rate * spread
        )
        spread = centred(none, flux_x, 1) + centred(none, unpacked(corner, 1), 0)
        level_cols = cols_o[step, 2] + cols_o[step, 3] * (
            uplift * seafloor[step, 2] - ocean_rate * spread
        )
        slope_x = centred(level, level_cols, 1)
        slope_y = centred(level, level_rows, 0)
        around_x = around(flux_x, halo_oy[step, 0], cols_o[step, 0])
        around_y = around(flux_y, halo_oy[step, 1], cols_o[step, 1])
        pull = ocean_rate * depth[...]
        sea[step + 1, 1] = wet * (flux_x - pull * slope_x + viscous * around_x)
        sea[step + 1, 2] = wet * (flux_y - pull * slope_y + viscous * around_y)

    for count, place in ((9 * 8 * layers, 0), (8 * layers, 1), (6 * 8, 2)):
        rows_done(count, load_sem.at[place])
    speeds = (speed_a, speed_b, speed_c)
    stresses = (stress_a, stress_b, stress_b)

    def first_push(pair, carry):
        for sub in range(2):
            push_chunk(0, pair, sub, stress_a, speed_a)
        return carry

    lax.fori_loop(0, 2, first_push, 0)
    ocean_prepare(0)

    peers = sum(there.astype(jnp.int32) for there in (*inside_x, *inside_y, *inside_d))
    pl.semaphore_wait(barrier, peers)

    def first_send(pair, carry):
        for sub in range(2):
            start_chunk(0, 2 * pair + sub)
        start_pair(0, pair)
        return carry

    def paced(pair, carry):
        first_send(pair - 2, carry)
        return first_push(pair, carry)

    lax.fori_loop(2, pairs, paced, 0)
    lax.fori_loop(pairs - 2, pairs, first_send, 0)
    rows_done(2 * 8 * layers, load_sem.at[3])

    for step in range(STEPS):
        last = step == STEPS - 1
        speed_old, speed_new = speeds[step], speeds[step + 1]
        stress_old, stress_new = stresses[step], stresses[step + 1]

        def join_of(pair, sub):
            rows_arrive(step, 2 * pair + sub)
            join_chunk(step, pair, sub, speed_new)

        def stress_of(pair, sub, pressed=True):
            halo_chunk(step, pair, sub)
            stress_chunk(step, pair, sub, speed_new, stress_old, stress_new, pressed)

        def push_of(pair, sub):
            if not last:
                push_chunk(step + 1, pair, sub, stress_new, speed_new)
                start_chunk(step + 1, 2 * pair + sub)
                if sub == 1:
                    start_pair(step + 1, pair)

        columns_arrive(step, 0)
        join_of(0, 0)
        join_of(0, 1)
        corners_arrive(step, 0)
        stress_of(0, 0, False)
        join_of(1, 0)
        stress_of(0, 1, False)
        columns_arrive(step, 1)
        corners_arrive(step, 1)
        join_of(1, 1)
        ocean_level(step)
        press_late(step, stress_new)
        stress_of(1, 0)
        push_of(0, 0)
        push_of(0, 1)
        for pair in range(2, pairs):
            join_of(pair, 0)
            stress_of(pair - 1, 1)
            push_of(pair - 1, 0)
            if pair == 2:
                ocean_flux(step)
                if not last:
                    ocean_prepare(step + 1)
            corners_arrive(step, pair)
            join_of(pair, 1)
            stress_of(pair, 0)
            push_of(pair - 1, 1)
        stress_of(pairs - 1, 1)
        push_of(pairs - 1, 0)
        push_of(pairs - 1, 1)

    for item in range(3):
        ocean_out[item] = sea[STEPS, item]
    drain()


def hand_on(waves, sea, waves_out, sea_out, sem):
    copies = [
        pltpu.make_async_copy(waves, waves_out, sem.at[0]),
        pltpu.make_async_copy(sea, sea_out, sem.at[1]),
    ]
    for copy in copies:
        copy.start()
    for copy in copies:
        copy.wait()


def solution(mesh):
    counts = (mesh.shape["gx"], mesh.shape["gy"])

    def local(*arrays):
        fields, ocean = arrays[0], arrays[4]
        layers = fields.shape[1]
        chunks, pairs = layers // CHUNK, layers // PACK
        f32, dma = jnp.float32, pltpu.SemaphoreType.DMA
        cube = (layers, *TILE)
        padded = (layers + 4, *TILE)
        waves, sea = pl.pallas_call(
            functools.partial(kernel, counts),
            out_shape=(pltpu.VMEM(fields.shape, f32), pltpu.VMEM(ocean.shape, f32)),
            in_specs=[pl.BlockSpec(memory_space=pl.ANY)] * 8,
            out_specs=(
                pl.BlockSpec(memory_space=pltpu.VMEM),
                pl.BlockSpec(memory_space=pltpu.VMEM),
            ),
            scratch_shapes=[
                pltpu.VMEM((9, *padded), f32),
                pltpu.VMEM((6, *padded), f32),
                pltpu.VMEM((3, *padded), f32),
                pltpu.VMEM((3, *padded), f32),
                pltpu.VMEM(cube, f32),
                pltpu.VMEM(cube, f32),
                pltpu.VMEM(cube, f32),
                pltpu.VMEM((STEPS + 1, 3, *TILE), f32),
                pltpu.VMEM(TILE, f32),
                pltpu.VMEM(TILE, jnp.int32),
                pltpu.VMEM(TILE, jnp.int32),
                pltpu.VMEM((STEPS, *TILE), f32),
                pltpu.VMEM((STEPS, 3, *cube), f32),
                pltpu.VMEM((STEPS, 3, *cube), f32),
                pltpu.VMEM((STEPS, pairs, 3, *TILE), f32),
                pltpu.VMEM((STEPS, 5, *TILE), f32),
                pltpu.VMEM((STEPS, *TILE), f32),
                pltpu.VMEM((STEPS, 3, *cube), f32),
                pltpu.VMEM((STEPS, 3, *cube), f32),
                pltpu.VMEM(cube, f32),
                pltpu.VMEM((STEPS, 2, pairs, 2, *TILE), f32),
                pltpu.VMEM((STEPS, 4, pairs, *TILE), f32),
                pltpu.VMEM((STEPS, 5, *TILE), f32),
                pltpu.VMEM((STEPS, 2, *TILE), f32),
                pltpu.VMEM((STEPS, 4, *TILE), f32),
                pltpu.VMEM((3, *cube), f32),
                pltpu.VMEM((STEPS, pairs, *TILE), f32),
                pltpu.VMEM((STEPS, 5, *TILE), f32),
                pltpu.VMEM((STEPS, 3, *TILE), f32),
                pltpu.VMEM((2, *TILE), f32),
                pltpu.VMEM((9 * layers * 8, 128), f32),
                dma((4,)),
                dma((2,)),
                dma((STEPS, 2, chunks)),
                dma((2,)),
                dma((STEPS, 2, 2)),
                dma((4,)),
                dma((STEPS, 4, pairs)),
            ],
            compiler_params=pltpu.CompilerParams(
                collective_id=0, has_side_effects=True, vmem_limit_bytes=60 << 20
            ),
            name="waves",
        )(*arrays)
        return pl.pallas_call(
            hand_on,
            out_shape=(
                jax.ShapeDtypeStruct(fields.shape, f32),
                jax.ShapeDtypeStruct(ocean.shape, f32),
            ),
            in_specs=[pl.BlockSpec(memory_space=pltpu.VMEM)] * 2,
            out_specs=(pl.BlockSpec(memory_space=pl.ANY), pl.BlockSpec(memory_space=pl.ANY)),
            scratch_shapes=[dma((2,))],
            compiler_params=pltpu.CompilerParams(vmem_limit_bytes=12 << 20),
            name="hand_on",
        )(waves, sea)

    flat = P("gy", "gx")
    deep = P(None, "gy", "gx")
    in_specs = (P(None, None, "gy", "gx"), deep, deep, deep, deep, flat, flat, flat)
    out_specs = (P(None, None, "gy", "gx"), deep)
    return jax.shard_map(local, mesh=mesh, in_specs=in_specs, out_specs=out_specs, check_vma=False)
```
